256 devices in a mesh: chan: 8 (over x, y_lo), tile: 32 (over y_hi, z, core).
Axes of the slice: x: 4, y: 4 (y_hi: 2, y_lo: 2; y = y_hi * 2 + y_lo), z: 8, core: 2. Of those that a mesh axis runs over, the one named last changes fastest.
Arguments:
- pixels: bfloat16 [128, 256, 1024], P('tile', None, 'chan'), may hold values from -6 to 6
- conv_weight: bfloat16 [3, 3, 1024, 1024], P(None, None, 'tile', 'chan'), may hold values from -0.0625 to 0.0625
- conv_bias: float32 [1024], P('chan'), may hold values from -3 to 3
- depth_weight: float32 [7, 7, 1024], P(None, None, 'chan'), may hold values from -0.875 to 0.875
- depth_bias: float32 [1024], P('chan'), may hold values from -3 to 3
Outputs:
- features: bfloat16 [128, 256, 1024], P('tile', None, 'chan')
The draws below stay inside these ranges and needn't reach their ends.
All inputs are finite; a program needn't handle non-finite values.
Results may differ from the reference program's by a relative error of at most 0.0043.
Values may be sent and summed in bfloat16 or wider, within the bound.
No kernel may reach another device: no remote copies, remote signals or barrier semaphores. Data moves between devices by JAX's collectives and lax.ppermute only.
A program may use at most 64 MiB of HBM per device.

```python
import jax
import jax.numpy as jnp
from jax import lax

CHANNELS = 1024
COLUMNS = 256
HEIGHT = 128


def level_of(key, extent, cuts, smallest, high):
    level = 1.0
    for axis_at, parts in cuts:
        heights = jax.random.uniform(jax.random.fold_in(jax.random.fold_in(key, 6), axis_at), (parts,), jnp.float32, smallest / len(cuts), high / len(cuts))
        level = level * jnp.repeat(jnp.exp(heights), extent[axis_at] // parts).reshape((-1,) + (1,) * (len(extent) - 1 - axis_at))
    return level


def scatter_about(key, shape, deviation, bound, shards=(), held_as=jnp.bfloat16):
    factor_of = level_of(key, shape, shards, -0.22, 0.18) if shards else 1.0
    result = jax.random.normal(key, shape, jnp.float32) * deviation * factor_of
    return jnp.minimum(jnp.maximum(result, -bound), bound).astype(held_as)


def setup_inputs(seed: int = 0) -> dict:
    seeds = jax.random.split(jax.random.key(seed), 6)
    pixels = scatter_about(seeds[0], (HEIGHT, COLUMNS, CHANNELS), 1.0, 6.0, ((0, 32), (2, 8)))
    conv_weight = scatter_about(seeds[1], (3, 3, CHANNELS, CHANNELS), (9 * CHANNELS) ** -0.5, 0.0625, ((2, 32), (3, 8)))
    conv_bias = scatter_about(seeds[2], (CHANNELS,), 0.5, 3.0, ((0, 8),), jnp.float32)
    depth_weight = scatter_about(seeds[3], (7, 7, CHANNELS), 49 ** -0.5, 0.875, ((2, 8),), jnp.float32)
    depth_bias = scatter_about(seeds[4], (CHANNELS,), 0.5, 3.0, ((0, 8),), jnp.float32)
    return dict(pixels=pixels, conv_weight=conv_weight, conv_bias=conv_bias, depth_weight=depth_weight, depth_bias=depth_bias)


def reference(pixels, conv_weight, conv_bias, depth_weight, depth_bias):
    convolved = lax.conv_general_dilated(pixels[None], conv_weight, (1, 1), ((1, 1), (1, 1)), dimension_numbers=("NHWC", "HWIO", "NHWC"), preferred_element_type=jnp.float32)[0]
    hidden = jax.nn.relu(convolved + conv_bias).astype(jnp.bfloat16)
    filters = depth_weight.reshape(7, 7, 1, CHANNELS)
    depthwise = lax.conv_general_dilated(hidden.astype(jnp.float32)[None], filters, (1, 1), ((3, 3), (3, 3)), dimension_numbers=("NHWC", "HWIO", "NHWC"), feature_group_count=CHANNELS, precision=lax.Precision.HIGHEST)[0]
    return (depthwise + depth_bias).astype(jnp.bfloat16)
```

```python
import jax
import jax.numpy as jnp
from jax import lax
from jax.experimental import pallas as pl
from jax.experimental.pallas import tpu as pltpu
from jax.sharding import PartitionSpec as P


ROWS, COLS, CH = 4, 256, 128
PIX = ROWS * COLS


def move_chan(block, partner):
    pairs = []
    for index in range(8):
        x, y = partner(index // 2, index % 2)
        pairs.append((index, 2 * x + y))
    return lax.ppermute(block, "chan", pairs)


def move_tile(block, partner):
    pairs = []
    for index in range(32):
        y, z, core = partner(index // 16, (index // 2) % 8, index % 2)
        pairs.append((index, (y * 8 + z % 8) * 2 + core))
    return lax.ppermute(block, "tile", pairs)


def over_y(x, y):
    return x, 1 - y


def over_a(x, y):
    return x ^ 1, y


def over_b(x, y):
    return (x + 1 if x % 2 else x - 1) % 4, y


def along_z(block, offset):
    return move_tile(block, lambda y, z, core: (y, z - offset, core))


def conv_kernel(*refs):
    p0, p_y, p_a, p_b, p_ya, p_ab, p_by, t0, t1, t2, w_own, w_other, bias, up, down, own, xs, ws, acc, sems = refs
    chan, tile = lax.axis_index("chan"), lax.axis_index("tile")
    x, y = chan // 2, chan % 2
    y_hi, z, core = tile // 16, (tile // 2) % 8, tile % 2
    xa = x + 1 - 2 * (x % 2)
    xb = (x + 3 + 2 * (x % 2)) % 4
    xc = (x + 2) % 4
    copies = []

    def copy(src, dst):
        copies.append(pltpu.make_async_copy(src, dst, sems.at[len(copies)]))
        copies[-1].start()

    def columns(index):
        return pl.ds(pl.multiple_of(index * CH, CH), CH)

    for block, at_x, at_y in (
        (p0, x, y), (p_y, x, 1 - y), (p_a, xa, y), (p_b, xb, y),
        (p_ya, xa, 1 - y), (p_ab, xc, y), (p_by, xb, 1 - y),
    ):
        copy(block, xs.at[:, columns(2 * at_x + at_y)])
    far = columns(2 * xc + 1 - y)
    copy(t0, xs.at[pl.ds(0, 336), far])
    copy(t1, xs.at[pl.ds(336, 336), far])
    copy(t2, xs.at[pl.ds(672, 352), far])
    for source, at_core in ((w_own, core), (w_other, 1 - core)):
        for slot in range(16):
            at_y, at_z = (y_hi + slot // 8) % 2, (z + slot % 8) % 8
            index = (at_y * 8 + at_z) * 2 + at_core
            copy(source.at[slot], ws.at[:, pl.ds(pl.multiple_of(index * 32, 32), 32), :])
    for each in copies:
        each.wait()

    groups = (((0, 0), (0, 1)), ((0, 2), (2, 0)), ((2, 1), (2, 2)), ((1, 0), (1, 1)), ((1, 2),))
    for taps in groups:
        filters = [ws[3 * a + b] for a, b in taps]
        rhs = jnp.concatenate(filters, axis=1) if len(taps) > 1 else filters[0]
        result = jnp.dot(xs[...], rhs, preferred_element_type=jnp.float32)
        for at, (a, b) in enumerate(taps):
            part = result[:, at * CH : (at + 1) * CH]
            if a == 0:
                acc[b, 512:1536, :] = part
            elif a == 2:
                acc[b, 0:512, :] = part[0:512]
                acc[b, 512:1024, :] += part[512:1024]
            else:
                acc[b, 256:1280, :] += part

    column = lax.broadcasted_iota(jnp.int32, (COLS, CH), 0)

    def row_sum(row):
        rows = slice((row + 1) * COLS, (row + 2) * COLS)
        left = jnp.where(column == 0, 0.0, pltpu.roll(acc[0, rows, :], 1, 0))
        right = jnp.where(column == COLS - 1, 0.0, pltpu.roll(acc[2, rows, :], COLS - 1, 0))
        return acc[1, rows, :] + left + right

    for slot, row in enumerate((-1, 0, 3, 4)):
        value = row_sum(row)
        own[slot] = value
        if slot < 2:
            up[slot] = value.astype(jnp.bfloat16)
        else:
            down[slot] = value.astype(jnp.bfloat16)
    for slot, row in enumerate((1, 2)):
        value = jnp.maximum(row_sum(row) + bias[...], 0.0).astype(jnp.bfloat16)
        up[2 + slot] = value
        down[slot] = value


def depth_kernel(own, up, above, below, bias, weight, depth_bias, out, hidden):
    tile = lax.axis_index("tile")
    has_above = (tile > 0).astype(jnp.float32)
    has_below = (tile < 31).astype(jnp.float32)
    f32 = jnp.float32
    pad = jnp.zeros((10, 8, CH), f32)
    hidden[:, 0:8, :] = pad
    hidden[:, 264:272, :] = pad

    def activate(value):
        return jnp.maximum(value + bias[...], 0.0).astype(jnp.bfloat16).astype(f32)

    rows = (
        above[0].astype(f32) * has_above,
        above[1].astype(f32) * has_above,
        activate(above[2].astype(f32) + own[0]) * has_above,
        activate(own[1] + above[3].astype(f32)),
        up[2].astype(f32),
        up[3].astype(f32),
        activate(own[2] + below[0].astype(f32)),
        activate(below[1].astype(f32) + own[3]) * has_below,
        below[2].astype(f32) * has_below,
        below[3].astype(f32) * has_below,
    )
    for at, value in enumerate(rows):
        hidden[at, 8:264, :] = value

    width = 32

    def strip(step, _):
        start = pl.multiple_of(step * width, width)
        sums = [jnp.zeros((width, CH), f32) + depth_bias[...] for _ in range(ROWS)]
        for at in range(10):
            wide = hidden[at, pl.ds(start, width + 16), :]
            for b in range(7):
                value = wide[5 + b : 5 + b + width]
                for row in range(ROWS):
                    a = at - row
                    if 0 <= a < 7:
                        sums[row] = sums[row] + value * weight[a, b : b + 1, :]
        for row in range(ROWS):
            out[row, pl.ds(start, width), :] = sums[row].astype(jnp.bfloat16)
        return 0

    lax.fori_loop(0, COLS // width, strip, 0)


def gather_all(pixels, weight):
    p0 = pixels.reshape(PIX, CH)
    w0 = weight.reshape(9, 32, CH)
    p_y, p_a, p_b = move_chan(p0, over_y), move_chan(p0, over_a), move_chan(p0, over_b)
    wb0 = move_tile(w0, lambda y, z, core: (1 - y, z, core))
    wa = {0: w0}
    for offset in (1, -1, 2, -2):
        wa[offset] = along_z(w0, offset)
    p_ya, p_ab, p_by = move_chan(p_a, over_y), move_chan(p_b, over_a), move_chan(p_y, over_b)
    wb = {0: wb0}
    for sign in (1, -1):
        both = along_z(jnp.stack([wa[2 * sign], wb0]), sign)
        wa[3 * sign], wb[sign] = both[0], both[1]
    plus = along_z(jnp.concatenate([wb0, wa[2][:5]]), 2)
    minus = along_z(jnp.concatenate([wb0, wa[-2][5:]]), -2)
    wb[2], wb[-2] = plus[:9], minus[:9]
    wa4 = (plus[9:], minus[9:])
    far = (
        move_chan(p_ab[0:336], over_y),
        move_chan(p_by[336:672], over_a),
        move_chan(p_ya[672:1024], over_b),
    )
    wb[3], wb[-3] = along_z(wb[2], 1), along_z(wb[-2], -1)
    wb4 = (along_z(wb[2][:5], 2), along_z(wb[-2][5:], -2))
    parts = []
    for ring, fourth in ((wa, wa4), (wb, wb4)):
        parts += [ring[0], ring[1], ring[2], ring[3], *fourth, ring[-3], ring[-2], ring[-1]]
    own = jnp.concatenate(parts).reshape(16, 9, 32, CH)
    other = move_tile(own, lambda y, z, core: (y, z, 1 - core))
    return (p0, p_y, p_a, p_b, p_ya, p_ab, p_by, *far), own, other


def body(pixels, conv_weight, conv_bias, depth_weight, depth_bias):
    blocks, w_own, w_other = gather_all(pixels, conv_weight)
    anywhere, vmem = pl.BlockSpec(memory_space=pl.ANY), pl.BlockSpec(memory_space=pltpu.VMEM)
    message = jax.ShapeDtypeStruct((4, COLS, CH), jnp.bfloat16)
    conv_bias = conv_bias.reshape(1, CH)
    up, down, own = pl.pallas_call(
        conv_kernel,
        out_shape=(message, message, jax.ShapeDtypeStruct((4, COLS, CH), jnp.float32)),
        in_specs=[anywhere] * 12 + [vmem],
        out_specs=(vmem, vmem, vmem),
        scratch_shapes=[
            pltpu.VMEM((PIX, 8 * CH), jnp.bfloat16),
            pltpu.VMEM((9, 8 * CH, CH), jnp.bfloat16),
            pltpu.VMEM((3, 6 * COLS, CH), jnp.float32),
            pltpu.SemaphoreType.DMA((42,)),
        ],
        compiler_params=pltpu.CompilerParams(vmem_limit_bytes=40 << 20),
        cost_estimate=pl.CostEstimate(flops=2 * PIX * 9 * 1024 * CH, bytes_accessed=6 << 20, transcendentals=0),
        name="conv",
    )(*blocks, w_own, w_other, conv_bias)
    below = lax.ppermute(up, "tile", [(i, i - 1) for i in range(1, 32)])
    above = lax.ppermute(down, "tile", [(i, i + 1) for i in range(31)])
    return pl.pallas_call(
        depth_kernel,
        out_shape=jax.ShapeDtypeStruct((ROWS, COLS, CH), jnp.bfloat16),
        in_specs=[vmem] * 7,
        out_specs=vmem,
        scratch_shapes=[pltpu.VMEM((10, COLS + 16, CH), jnp.float32)],
        compiler_params=pltpu.CompilerParams(vmem_limit_bytes=20 << 20),
        cost_estimate=pl.CostEstimate(flops=2 * PIX * 49 * CH, bytes_accessed=2 << 20, transcendentals=0),
        name="depth",
    )(own, up, above, below, conv_bias, depth_weight, depth_bias.reshape(1, CH))


def solution(mesh):
    in_specs = (
        P("tile", None, "chan"),
        P(None, None, "tile", "chan"),
        P("chan"),
        P(None, None, "chan"),
        P("chan"),
    )
    out_specs = P("tile", None, "chan")
    return jax.shard_map(body, mesh=mesh, in_specs=in_specs, out_specs=out_specs, check_vma=False)
```

```python
import jax
import jax.numpy as jnp
from jax import lax
from jax.experimental import pallas as pl
from jax.experimental.pallas import tpu as pltpu
from jax.sharding import PartitionSpec as P


ROWS, COLS, CH = 4, 256, 128
PIX = ROWS * COLS


def move_chan(block, partner):
    pairs = []
    for index in range(8):
        x, y = partner(index // 2, index % 2)
        pairs.append((index, 2 * x + y))
    return lax.ppermute(block, "chan", pairs)


def move_tile(block, partner):
    pairs = []
    for index in range(32):
        y, z, core = partner(index // 16, (index // 2) % 8, index % 2)
        pairs.append((index, (y * 8 + z % 8) * 2 + core))
    return lax.ppermute(block, "tile", pairs)


def over_y(x, y):
    return x, 1 - y


def over_a(x, y):
    return x ^ 1, y


def over_b(x, y):
    return (x + 1 if x % 2 else x - 1) % 4, y


def over_za(y, z, core):
    return y, z ^ 1, core


def over_zb(y, z, core):
    return y, (z + 1 if z % 2 else z - 1) % 8, core


def over_hi(y, z, core):
    return 1 - y, z, core


def over_core(y, z, core):
    return y, z, 1 - core


PIECES = (
    ((0, 0, 0, 0, 9),),
    ((0, 0, 1, 0, 9),),
    ((0, 0, -1, 0, 9),),
    ((0, 1, 0, 0, 9),),
    ((0, 1, 1, 0, 9), (9, 0, 2, 0, 9)),
    ((0, 0, -2, 0, 9), (9, 1, -1, 0, 9)),
    ((0, 0, 3, 0, 9), (9, 1, 2, 0, 9)),
    ((0, 1, -2, 0, 9), (9, 0, -3, 0, 9)),
    ((0, 1, 3, 0, 9), (9, 0, 4, 0, 4)),
    ((0, 0, 4, 4, 5), (5, 1, -3, 0, 9)),
    ((0, 1, 4, 0, 4),),
    ((0, 1, 4, 4, 5),),
)
LENGTHS = (9, 9, 9, 9, 18, 18, 18, 18, 13, 14, 4, 5)
PACKS = ((0, 1, 2, 3, 4, 5), (6, 7, 8, 9), (10, 11))


def conv_kernel(*refs):
    blocks, own_w, packs = refs[:10], refs[10:22], refs[22:25]
    bias, up, down, own, xs, ws, acc, sems = refs[25:]
    chan, tile = lax.axis_index("chan"), lax.axis_index("tile")
    x, y = chan // 2, chan % 2
    y_hi, z, core = tile // 16, (tile // 2) % 8, tile % 2
    xa = x + 1 - 2 * (x % 2)
    xb = (x + 3 + 2 * (x % 2)) % 4
    xc = (x + 2) % 4
    side = 1 - 2 * (z % 2)
    copies = []

    def copy(src, dst):
        copies.append(pltpu.make_async_copy(src, dst, sems.at[len(copies)]))
        copies[-1].start()

    def columns(index):
        return pl.ds(pl.multiple_of(index * CH, CH), CH)

    for block, (at_x, at_y) in zip(
        blocks, ((x, y), (x, 1 - y), (xa, y), (xb, y), (xa, 1 - y), (xc, y), (xb, 1 - y))
    ):
        copy(block, xs.at[:, columns(2 * at_x + at_y)])
    far = columns(2 * xc + 1 - y)
    for block, first, count in zip(blocks[7:], (0, 336, 672), (336, 336, 352)):
        copy(block, xs.at[pl.ds(first, count), far])

    def place(array, offset, pieces, at_core):
        for row, flip, steps, first, taps in pieces:
            index = (((y_hi + flip) % 2) * 8 + (z + steps * side + 8) % 8) * 2 + at_core
            rows = pl.ds(pl.multiple_of(index * 32, 32), 32)
            copy(array.at[pl.ds(offset + row, taps)], ws.at[pl.ds(first, taps), rows, :])

    for array, pieces in zip(own_w, PIECES):
        place(array, 0, pieces, core)
    for pack, members in zip(packs, PACKS):
        offset = 0
        for member in members:
            place(pack, offset, PIECES[member], 1 - core)
            offset += LENGTHS[member]
    for each in copies:
        each.wait()

    groups = (((0, 0), (0, 1)), ((0, 2), (2, 0)), ((2, 1), (2, 2)), ((1, 0), (1, 1)), ((1, 2),))
    for taps in groups:
        filters = [ws[3 * a + b] for a, b in taps]
        rhs = jnp.concatenate(filters, axis=1) if len(taps) > 1 else filters[0]
        result = jnp.dot(xs[...], rhs, preferred_element_type=jnp.float32)
        for at, (a, b) in enumerate(taps):
            part = result[:, at * CH : (at + 1) * CH]
            if a == 0:
                acc[b, 512:1536, :] = part
            elif a == 2:
                acc[b, 0:512, :] = part[0:512]
                acc[b, 512:1024, :] += part[512:1024]
            else:
                acc[b, 256:1280, :] += part

    column = lax.broadcasted_iota(jnp.int32, (COLS, CH), 0)

    def row_sum(row):
        rows = slice((row + 1) * COLS, (row + 2) * COLS)
        left = jnp.where(column == 0, 0.0, pltpu.roll(acc[0, rows, :], 1, 0))
        right = jnp.where(column == COLS - 1, 0.0, pltpu.roll(acc[2, rows, :], COLS - 1, 0))
        return acc[1, rows, :] + left + right

    for slot, row in enumerate((-1, 0, 3, 4)):
        value = row_sum(row)
        own[slot] = value
        if slot < 2:
            up[slot] = value.astype(jnp.bfloat16)
        else:
            down[slot] = value.astype(jnp.bfloat16)
    for slot, row in enumerate((1, 2)):
        value = jnp.maximum(row_sum(row) + bias[...], 0.0).astype(jnp.bfloat16)
        up[2 + slot] = value
        down[slot] = value


def depth_kernel(own, up, above, below, bias, weight, depth_bias, out, hidden):
    tile = lax.axis_index("tile")
    has_above = (tile > 0).astype(jnp.float32)
    has_below = (tile < 31).astype(jnp.float32)
    f32 = jnp.float32
    pad = jnp.zeros((10, 8, CH), f32)
    hidden[:, 0:8, :] = pad
    hidden[:, 264:272, :] = pad

    def activate(value):
        return jnp.maximum(value + bias[...], 0.0).astype(jnp.bfloat16).astype(f32)

    rows = (
        above[0].astype(f32) * has_above,
        above[1].astype(f32) * has_above,
        activate(above[2].astype(f32) + own[0]) * has_above,
        activate(own[1] + above[3].astype(f32)),
        up[2].astype(f32),
        up[3].astype(f32),
        activate(own[2] + below[0].astype(f32)),
        activate(below[1].astype(f32) + own[3]) * has_below,
        below[2].astype(f32) * has_below,
        below[3].astype(f32) * has_below,
    )
    for at, value in enumerate(rows):
        hidden[at, 8:264, :] = value

    width = 32

    def strip(step, _):
        start = pl.multiple_of(step * width, width)
        sums = [jnp.zeros((width, CH), f32) + depth_bias[...] for _ in range(ROWS)]
        for at in range(10):
            wide = hidden[at, pl.ds(start, width + 16), :]
            for b in range(7):
                value = wide[5 + b : 5 + b + width]
                for row in range(ROWS):
                    a = at - row
                    if 0 <= a < 7:
                        sums[row] = sums[row] + value * weight[a, b : b + 1, :]
        for row in range(ROWS):
            out[row, pl.ds(start, width), :] = sums[row].astype(jnp.bfloat16)
        return 0

    lax.fori_loop(0, COLS // width, strip, 0)


def gather_all(pixels, weight):
    p0 = pixels.reshape(PIX, CH)
    w0 = weight.reshape(9, 32, CH)

    h0 = move_tile(w0, over_hi)
    a1, b1 = move_tile(w0, over_za), move_tile(w0, over_zb)
    p_y, p_a, p_b = move_chan(p0, over_y), move_chan(p0, over_a), move_chan(p0, over_b)
    a2 = move_tile(jnp.concatenate([h0, b1]), over_za)
    b2 = move_tile(jnp.concatenate([a1, h0]), over_zb)
    p_ya, p_ab, p_by = move_chan(p_a, over_y), move_chan(p_b, over_a), move_chan(p_y, over_b)
    a3, b3 = move_tile(b2, over_za), move_tile(a2, over_zb)
    a4, b4 = move_tile(b3[0:13], over_za), move_tile(a3[4:18], over_zb)
    far = (
        move_chan(p_ab[0:336], over_y),
        move_chan(p_by[336:672], over_a),
        move_chan(p_ya[672:1024], over_b),
    )
    a5, b5 = move_tile(b4[5:9], over_za), move_tile(a4[4:9], over_zb)
    own = (w0, a1, b1, h0, a2, b2, a3, b3, a4, b4, a5, b5)
    packs = tuple(
        move_tile(jnp.concatenate([own[member] for member in members]), over_core)
        for members in PACKS
    )
    return (p0, p_y, p_a, p_b, p_ya, p_ab, p_by, *far), own, packs


def body(pixels, conv_weight, conv_bias, depth_weight, depth_bias):
    blocks, own_w, packs = gather_all(pixels, conv_weight)
    anywhere, vmem = pl.BlockSpec(memory_space=pl.ANY), pl.BlockSpec(memory_space=pltpu.VMEM)
    message = jax.ShapeDtypeStruct((4, COLS, CH), jnp.bfloat16)
    conv_bias = conv_bias.reshape(1, CH)
    up, down, own = pl.pallas_call(
        conv_kernel,
        out_shape=(message, message, jax.ShapeDtypeStruct((4, COLS, CH), jnp.float32)),
        in_specs=[anywhere] * 25 + [vmem],
        out_specs=(vmem, vmem, vmem),
        scratch_shapes=[
            pltpu.VMEM((PIX, 8 * CH), jnp.bfloat16),
            pltpu.VMEM((9, 8 * CH, CH), jnp.bfloat16),
            pltpu.VMEM((3, 6 * COLS, CH), jnp.float32),
            pltpu.SemaphoreType.DMA((46,)),
        ],
        compiler_params=pltpu.CompilerParams(vmem_limit_bytes=40 << 20),
        cost_estimate=pl.CostEstimate(flops=2 * PIX * 9 * 1024 * CH, bytes_accessed=6 << 20, transcendentals=0),
        name="conv",
    )(*blocks, *own_w, *packs, conv_bias)
    below = lax.ppermute(up, "tile", [(i, i - 1) for i in range(1, 32)])
    above = lax.ppermute(down, "tile", [(i, i + 1) for i in range(31)])
    return pl.pallas_call(
        depth_kernel,
        out_shape=jax.ShapeDtypeStruct((ROWS, COLS, CH), jnp.bfloat16),
        in_specs=[vmem] * 7,
        out_specs=vmem,
        scratch_shapes=[pltpu.VMEM((10, COLS + 16, CH), jnp.float32)],
        compiler_params=pltpu.CompilerParams(vmem_limit_bytes=20 << 20),
        cost_estimate=pl.CostEstimate(flops=2 * PIX * 49 * CH, bytes_accessed=2 << 20, transcendentals=0),
        name="depth",
    )(own, up, above, below, conv_bias, depth_weight, depth_bias.reshape(1, CH))


def solution(mesh):
    in_specs = (
        P("tile", None, "chan"),
        P(None, None, "tile", "chan"),
        P("chan"),
        P(None, None, "chan"),
        P("chan"),
    )
    out_specs = P("tile", None, "chan")
    return jax.shard_map(body, mesh=mesh, in_specs=in_specs, out_specs=out_specs, check_vma=False)
```

```python
import jax
import jax.numpy as jnp
from jax import lax
from jax.experimental import pallas as pl
from jax.experimental.pallas import tpu as pltpu
from jax.sharding import PartitionSpec as P


ROWS, COLS, CH = 4, 256, 128
PIX = ROWS * COLS


def over_a(x):
    return x ^ 1


def over_b(x):
    return (x + 1 if x % 2 else x - 1) % 4


def move(block, partner):
    pairs = []
    for chan in range(8):
        for tile in range(32):
            x, y, hi, z, core = partner(chan // 2, chan % 2, tile // 16, (tile // 2) % 8, tile % 2)
            pairs.append((chan * 32 + tile, (2 * x + y) * 32 + (hi * 8 + z % 8) * 2 + core))
    return lax.ppermute(block, ("chan", "tile"), pairs)


def to_y(x, y, hi, z, core):
    return x, 1 - y, hi, z, core


def to_l(x, y, hi, z, core):
    return (over_b(x) if core else over_a(x)), y, hi, z, core


def to_m(x, y, hi, z, core):
    return (over_a(x) if core else over_b(x)), y, hi, z, core


def to_hi(x, y, hi, z, core):
    return x, y, 1 - hi, z, core


def to_core(x, y, hi, z, core):
    return x, y, hi, z, 1 - core


def to_next(x, y, hi, z, core):
    return x, y, hi, (z - 1 if core else z + 1), core


PIECES = (
    ((0, 0, 0),),
    ((0, 0, 1),),
    ((1, 0, 0),),
    ((1, 0, 1),),
    ((0, 1, 1), (0, 1, 0)),
    ((0, 2, 1), (0, 2, 0), (1, 1, 0), (1, 1, 1)),
    ((0, 3, 1), (0, 3, 0), (1, 2, 0), (1, 2, 1)),
    ((0, 4, 0), (1, 3, 0), (1, 3, 1)),
    ((1, 4, 0),),
)
OTHER_PIECES = (PIECES[4] + PIECES[5],) + PIECES[6:]


def conv_kernel(*refs):
    blocks, own_w, other_w = refs[:8], refs[8:17], refs[17:21]
    small, (outer, inner, mid, own, *params), (xs, ws, acc, up, down, sems) = refs[21:24], refs[24:31], refs[31:]
    bias = params[0]
    chan, tile = lax.axis_index("chan"), lax.axis_index("tile")
    x, y = chan // 2, chan % 2
    y_hi, z, core = tile // 16, (tile // 2) % 8, tile % 2
    turn = 1 - 2 * ((x + core) % 2)
    xl, xm, xf = (x + turn + 4) % 4, (x - turn + 4) % 4, (x + 2) % 4
    copies = []

    def copy(src, dst):
        copies.append(pltpu.make_async_copy(src, dst, sems.at[len(copies)]))
        copies[-1].start()

    places = ((x, y), (x, 1 - y), (xl, y), (xm, y), (xl, 1 - y), (xf, y), (xm, 1 - y), (xf, 1 - y))
    for block, (at_x, at_y) in zip(blocks, places):
        copy(block, xs.at[:, pl.ds(pl.multiple_of((2 * at_x + at_y) * CH, CH), CH)])

    def place(array, pieces, at_core):
        back = 1 - 2 * at_core
        for row, (flip, steps, other) in enumerate(pieces):
            at_z = (z - steps * back + 8) % 8
            index = (((y_hi + flip) % 2) * 8 + at_z) * 2 + (at_core + other) % 2
            rows = pl.ds(pl.multiple_of(index * 32, 32), 32)
            copy(array.at[pl.ds(9 * row, 9)], ws.at[:, rows, :])

    for array, pieces in zip(own_w, PIECES):
        place(array, pieces, core)
    for array, pieces in zip(other_w, OTHER_PIECES):
        place(array, pieces, 1 - core)
    for source, target in zip(small, params):
        copy(source, target)
    for each in copies:
        each.wait()

    groups = (((0, 0), (0, 1)), ((0, 2), (2, 0)), ((2, 1), (2, 2)), ((1, 0), (1, 1)), ((1, 2),))
    for taps in groups:
        filters = [ws[3 * a + b] for a, b in taps]
        rhs = jnp.concatenate(filters, axis=1) if len(taps) > 1 else filters[0]
        result = jnp.dot(xs[...], rhs, preferred_element_type=jnp.float32)
        for at, (a, b) in enumerate(taps):
            part = result[:, at * CH : (at + 1) * CH]
            if a == 0:
                acc[b, 512:1536, :] = part
            elif a == 2:
                acc[b, 0:512, :] = part[0:512]
                acc[b, 512:1024, :] += part[512:1024]
            else:
                acc[b, 256:1280, :] += part

    column = lax.broadcasted_iota(jnp.int32, (COLS, CH), 0)

    def row_sum(row):
        rows = slice((row + 1) * COLS, (row + 2) * COLS)
        left = jnp.where(column == 0, 0.0, pltpu.roll(acc[0, rows, :], 1, 0))
        right = jnp.where(column == COLS - 1, 0.0, pltpu.roll(acc[2, rows, :], COLS - 1, 0))
        return acc[1, rows, :] + left + right

    for slot, row in enumerate((-1, 0, 4, 3)):
        value = row_sum(row)
        own[slot] = value
        if slot < 2:
            up[slot] = value.astype(jnp.bfloat16)
        else:
            down[slot - 2] = value.astype(jnp.bfloat16)
    for slot, row in enumerate((1, 2)):
        value = jnp.maximum(row_sum(row) + bias[...], 0.0).astype(jnp.bfloat16)
        mid[slot] = value
        up[2 + slot] = value
        down[3 - slot] = value

    @pl.when(core == 0)
    def _():
        outer[...] = up[...]
        inner[...] = down[...]

    @pl.when(core == 1)
    def _():
        outer[...] = down[...]
        inner[...] = up[...]


def depth_kernel(own, mid, from_outer, from_inner, bias, depth_bias, weight, out, hidden):
    tile = lax.axis_index("tile")
    has_above = (tile > 0).astype(jnp.float32)
    has_below = (tile < 31).astype(jnp.float32)
    f32 = jnp.float32
    pad = jnp.zeros((10, 8, CH), f32)
    hidden[:, 0:8, :] = pad
    hidden[:, 264:272, :] = pad

    def activate(value):
        return jnp.maximum(value + bias[...], 0.0).astype(jnp.bfloat16).astype(f32)

    def fill(above, below):
        rows = (
            above[3].astype(f32) * has_above,
            above[2].astype(f32) * has_above,
            activate(above[1].astype(f32) + own[0]) * has_above,
            activate(own[1] + above[0].astype(f32)),
            mid[0].astype(f32),
            mid[1].astype(f32),
            activate(own[3] + below[0].astype(f32)),
            activate(below[1].astype(f32) + own[2]) * has_below,
            below[2].astype(f32) * has_below,
            below[3].astype(f32) * has_below,
        )
        for at, value in enumerate(rows):
            hidden[at, 8:264, :] = value

    @pl.when(tile % 2 == 0)
    def _():
        fill(from_outer, from_inner)

    @pl.when(tile % 2 == 1)
    def _():
        fill(from_inner, from_outer)

    width = 32

    def strip(step, _):
        start = pl.multiple_of(step * width, width)
        sums = [jnp.zeros((width, CH), f32) + depth_bias[...] for _ in range(ROWS)]
        for at in range(10):
            wide = hidden[at, pl.ds(start, width + 16), :]
            for b in range(7):
                value = wide[5 + b : 5 + b + width]
                for row in range(ROWS):
                    a = at - row
                    if 0 <= a < 7:
                        sums[row] = sums[row] + value * weight[a, b : b + 1, :]
        for row in range(ROWS):
            out[row, pl.ds(start, width), :] = sums[row].astype(jnp.bfloat16)
        return 0

    lax.fori_loop(0, COLS // width, strip, 0)


def gather_all(pixels, weight):
    p0 = pixels.reshape(PIX, CH)
    w0 = weight.reshape(9, 32, CH)
    h0 = move(w0, to_hi)
    w0_other = move(w0, to_core)
    r1 = move(jnp.concatenate([w0_other, w0]), to_next)
    p_y, p_l, p_m = move(p0, to_y), move(p0, to_l), move(p0, to_m)
    h0_other = move(h0, to_core)
    r2 = move(jnp.concatenate([r1, h0, h0_other]), to_next)
    p_ly, p_ml, p_ym = move(p_l, to_y), move(p_m, to_l), move(p_y, to_m)
    r3 = move(r2, to_next)
    o2 = move(jnp.concatenate([r1, r2]), to_core)
    r4 = move(r3[9:36], to_next)
    o3 = move(r3, to_core)
    p_far = move(p_ym, to_l)
    r5 = move(r4[9:18], to_next)
    o4 = move(r4, to_core)
    o5 = move(r5, to_core)
    blocks = (p0, p_y, p_l, p_m, p_ly, p_ml, p_ym, p_far)
    return blocks, (w0, w0_other, h0, h0_other, r1, r2, r3, r4, r5), (o2, o3, o4, o5)


def body(pixels, conv_weight, conv_bias, depth_weight, depth_bias):
    blocks, own_w, other_w = gather_all(pixels, conv_weight)
    anywhere, vmem = pl.BlockSpec(memory_space=pl.ANY), pl.BlockSpec(memory_space=pltpu.VMEM)
    f32, bf16 = jnp.float32, jnp.bfloat16
    message = jax.ShapeDtypeStruct((4, COLS, CH), bf16)
    outer, inner, mid, own, *params = pl.pallas_call(
        conv_kernel,
        out_shape=(
            message,
            message,
            jax.ShapeDtypeStruct((2, COLS, CH), bf16),
            jax.ShapeDtypeStruct((4, COLS, CH), f32),
            jax.ShapeDtypeStruct((1, CH), f32),
            jax.ShapeDtypeStruct((1, CH), f32),
            jax.ShapeDtypeStruct((7, 7, CH), f32),
        ),
        in_specs=[anywhere] * 24,
        out_specs=(vmem,) * 7,
        scratch_shapes=[
            pltpu.VMEM((PIX, 8 * CH), bf16),
            pltpu.VMEM((9, 8 * CH, CH), bf16),
            pltpu.VMEM((3, 6 * COLS, CH), f32),
            pltpu.VMEM((4, COLS, CH), bf16),
            pltpu.VMEM((4, COLS, CH), bf16),
            pltpu.SemaphoreType.DMA((43,)),
        ],
        compiler_params=pltpu.CompilerParams(vmem_limit_bytes=40 << 20),
        cost_estimate=pl.CostEstimate(flops=2 * PIX * 9 * 1024 * CH, bytes_accessed=6 << 20, transcendentals=0),
        name="conv",
    )(
        *blocks, *own_w, *other_w,
        conv_bias.reshape(1, CH), depth_bias.reshape(1, CH), depth_weight,
    )
    across = [(i, i + 1) for i in range(1, 31, 2)]
    from_outer = lax.ppermute(outer, "tile", across + [(j, i) for i, j in across])
    from_inner = lax.ppermute(inner, "tile", [(i, i ^ 1) for i in range(32)])
    return pl.pallas_call(
        depth_kernel,
        out_shape=jax.ShapeDtypeStruct((ROWS, COLS, CH), bf16),
        in_specs=[vmem] * 7,
        out_specs=vmem,
        scratch_shapes=[pltpu.VMEM((10, COLS + 16, CH), f32)],
        compiler_params=pltpu.CompilerParams(vmem_limit_bytes=20 << 20),
        cost_estimate=pl.CostEstimate(flops=2 * PIX * 49 * CH, bytes_accessed=2 << 20, transcendentals=0),
        name="depth",
    )(own, mid, from_outer, from_inner, *params)


def solution(mesh):
    in_specs = (
        P("tile", None, "chan"),
        P(None, None, "tile", "chan"),
        P("chan"),
        P(None, None, "chan"),
        P("chan"),
    )
    out_specs = P("tile", None, "chan")
    return jax.shard_map(body, mesh=mesh, in_specs=in_specs, out_specs=out_specs, check_vma=False)
```

```python
import jax
import jax.numpy as jnp
from jax import lax
from jax.experimental import pallas as pl
from jax.experimental.pallas import tpu as pltpu
from jax.sharding import PartitionSpec as P


ROWS, COLS, CH = 4, 256, 128
PIX = ROWS * COLS


def over_a(x):
    return x ^ 1


def over_b(x):
    return (x + 1 if x % 2 else x - 1) % 4


def move(block, partner):
    pairs = []
    for chan in range(8):
        for tile in range(32):
            x, y, hi, z, core = partner(chan // 2, chan % 2, tile // 16, (tile // 2) % 8, tile % 2)
            pairs.append((chan * 32 + tile, (2 * x + y) * 32 + (hi * 8 + z % 8) * 2 + core))
    return lax.ppermute(block, ("chan", "tile"), pairs)


def to_y(x, y, hi, z, core):
    return x, 1 - y, hi, z, core


def to_l(x, y, hi, z, core):
    return (over_b(x) if core else over_a(x)), y, hi, z, core


def to_m(x, y, hi, z, core):
    return (over_a(x) if core else over_b(x)), y, hi, z, core


def to_core(x, y, hi, z, core):
    return x, y, hi, z, 1 - core


def to_next(x, y, hi, z, core):
    return x, y, hi, (z - 1 if core else z + 1), core


TAPS = (((0, 0), (0, 1)), ((0, 2), (2, 0)), ((2, 1), (2, 2)), ((1, 0), (1, 1)), ((1, 2),))
EARLY = 6 * CH


def add_taps(pixels, filters, acc):
    for taps in TAPS:
        columns = [filters(3 * a + b) for a, b in taps]
        rhs = jnp.concatenate(columns, axis=1) if len(taps) > 1 else columns[0]
        result = jnp.dot(pixels(), rhs, preferred_element_type=jnp.float32)
        for at, (a, b) in enumerate(taps):
            part = result[:, at * CH : (at + 1) * CH]
            if a == 0:
                acc[b, 512:1536, :] = part
            elif a == 2:
                acc[b, 0:512, :] = part[0:512]
                acc[b, 512:1024, :] += part[512:1024]
            else:
                acc[b, 256:1280, :] += part


class Copies:
    def __init__(self, sems):
        self.sems, self.started = sems, []

    def start(self, src, dst):
        copy = pltpu.make_async_copy(src, dst, self.sems.at[len(self.started)])
        copy.start()
        self.started.append(copy)

    def wait(self):
        for copy in self.started:
            copy.wait()


def block_at(pair, half, z):
    return 2 * ((pair - z // 2 + 5) % 4) + half


def early_kernel(*refs):
    blocks, own_w, other_w, small = refs[:8], refs[8:12], refs[12:15], refs[15:18]
    (xs, ws, acc, *params), sems = refs[18:24], refs[24]
    chan, tile = lax.axis_index("chan"), lax.axis_index("tile")
    x, y = chan // 2, chan % 2
    z, core = (tile // 2) % 8, tile % 2
    turn = 1 - 2 * ((x + core) % 2)
    xl, xm, xf = (x + turn + 4) % 4, (x - turn + 4) % 4, (x + 2) % 4
    copies = Copies(sems)
    places = ((x, y), (x, 1 - y), (xl, y), (xm, y), (xl, 1 - y), (xf, y), (xm, 1 - y), (xf, 1 - y))
    for block, (at_x, at_y) in zip(blocks, places):
        index = 2 * at_x + at_y
        at = block_at(index % 4, index // 4, z)
        copies.start(block, xs.at[:, pl.ds(pl.multiple_of(at * CH, CH), CH)])

    def place(array, at_z):
        for half in range(2):
            for at_core in range(2):
                row = block_at(at_z // 2, half, z) * CH + (at_z % 2) * 64 + at_core * 32
                rows = pl.ds(pl.multiple_of(row, 32), 32)
                copies.start(array.at[pl.ds(9 * (2 * half + at_core), 9)], ws.at[:, rows, :])

    back = 1 - 2 * core
    for steps, array in enumerate(own_w):
        place(array, (z - steps * back + 8) % 8)
    for steps, array in enumerate(other_w):
        place(array, (z + (steps + 1) * back + 8) % 8)
    for source, target in zip(small, params):
        copies.start(source, target)
    copies.wait()
    add_taps(lambda: xs[:, 0:EARLY], lambda tap: ws[tap, 0:EARLY, :], acc)


def late_kernel(xs, ws_early, acc_early, last, bias, outer, inner, mid, own, ws, acc, up, down, sems):
    tile = lax.axis_index("tile")
    z, core = (tile // 2) % 8, tile % 2
    copies = Copies(sems)
    for half in range(2):
        rows = pl.ds(pl.multiple_of(half * CH + (1 - z % 2) * 64, 64), 64)
        early = pl.ds(pl.multiple_of(EARLY + half * CH + (1 - z % 2) * 64, 64), 64)
        copies.start(ws_early.at[:, early, :], ws.at[:, rows, :])
        for at_core in range(2):
            rows = pl.ds(pl.multiple_of(half * CH + (z % 2) * 64 + at_core * 32, 32), 32)
            copies.start(last.at[pl.ds(9 * (2 * half + at_core), 9)], ws.at[:, rows, :])
    copies.wait()
    add_taps(lambda: xs[:, EARLY : 8 * CH], lambda tap: ws[tap], acc)

    column = lax.broadcasted_iota(jnp.int32, (COLS, CH), 0)

    def row_sum(row):
        rows = slice((row + 1) * COLS, (row + 2) * COLS)
        total = [acc[b, rows, :] + acc_early[b, rows, :] for b in range(3)]
        left = jnp.where(column == 0, 0.0, pltpu.roll(total[0], 1, 0))
        right = jnp.where(column == COLS - 1, 0.0, pltpu.roll(total[2], COLS - 1, 0))
        return total[1] + left + right

    for slot, row in enumerate((-1, 0, 4, 3)):
        value = row_sum(row)
        own[slot] = value
        if slot < 2:
            up[slot] = value.astype(jnp.bfloat16)
        else:
            down[slot - 2] = value.astype(jnp.bfloat16)
    for slot, row in enumerate((1, 2)):
        value = jnp.maximum(row_sum(row) + bias[...], 0.0).astype(jnp.bfloat16)
        mid[slot] = value
        up[2 + slot] = value
        down[3 - slot] = value

    @pl.when(core == 0)
    def _():
        outer[...] = up[...]
        inner[...] = down[...]

    @pl.when(core == 1)
    def _():
        outer[...] = down[...]
        inner[...] = up[...]


def depth_kernel(own, mid, from_outer, from_inner, bias, depth_bias, weight, out, hidden):
    tile = lax.axis_index("tile")
    has_above = (tile > 0).astype(jnp.float32)
    has_below = (tile < 31).astype(jnp.float32)
    f32 = jnp.float32
    pad = jnp.zeros((10, 8, CH), f32)
    hidden[:, 0:8, :] = pad
    hidden[:, 264:272, :] = pad

    def activate(value):
        return jnp.maximum(value + bias[...], 0.0).astype(jnp.bfloat16).astype(f32)

    def fill(above, below):
        rows = (
            above[3].astype(f32) * has_above,
            above[2].astype(f32) * has_above,
            activate(above[1].astype(f32) + own[0]) * has_above,
            activate(own[1] + above[0].astype(f32)),
            mid[0].astype(f32),
            mid[1].astype(f32),
            activate(own[3] + below[0].astype(f32)),
            activate(below[1].astype(f32) + own[2]) * has_below,
            below[2].astype(f32) * has_below,
            below[3].astype(f32) * has_below,
        )
        for at, value in enumerate(rows):
            hidden[at, 8:264, :] = value

    @pl.when(tile % 2 == 0)
    def _():
        fill(from_outer, from_inner)

    @pl.when(tile % 2 == 1)
    def _():
        fill(from_inner, from_outer)

    width = 32

    def strip(step, _):
        start = pl.multiple_of(step * width, width)
        sums = [jnp.zeros((width, CH), f32) + depth_bias[...] for _ in range(ROWS)]
        for at in range(10):
            wide = hidden[at, pl.ds(start, width + 16), :]
            for b in range(7):
                value = wide[5 + b : 5 + b + width]
                for row in range(ROWS):
                    a = at - row
                    if 0 <= a < 7:
                        sums[row] = sums[row] + value * weight[a, b : b + 1, :]
        for row in range(ROWS):
            out[row, pl.ds(start, width), :] = sums[row].astype(jnp.bfloat16)
        return 0

    lax.fori_loop(0, COLS // width, strip, 0)


def gather_all(pixels, weight):
    p0 = pixels.reshape(PIX, CH)
    groups = [[(hi * 8 + z) * 2 + core for hi in range(2) for core in range(2)] for z in range(8)]
    four = jnp.broadcast_to(weight.reshape(1, 9, 32, CH), (4, 9, 32, CH)).reshape(36, 32, CH)
    w0 = lax.all_to_all(four, "tile", 0, 0, tiled=True, axis_index_groups=groups)
    w1 = move(w0, to_next)
    p_y, p_l, p_m = move(p0, to_y), move(p0, to_l), move(p0, to_m)
    w2 = move(w1, to_next)
    o1 = move(w1, to_core)
    p_ly, p_ml, p_ym = move(p_l, to_y), move(p_m, to_l), move(p_y, to_m)
    w3 = move(w2, to_next)
    o2 = move(w2, to_core)
    p_far = move(p_ym, to_l)
    w4 = move(w3, to_next)
    o3 = move(w3, to_core)
    return (p0, p_y, p_l, p_m, p_ly, p_ml, p_ym, p_far, w0, w1, w2, w3, o1, o2, o3), w4


def body(pixels, conv_weight, conv_bias, depth_weight, depth_bias):
    anywhere, vmem = pl.BlockSpec(memory_space=pl.ANY), pl.BlockSpec(memory_space=pltpu.VMEM)
    hbm = pl.BlockSpec(memory_space=pltpu.HBM)
    f32, bf16 = jnp.float32, jnp.bfloat16
    message = jax.ShapeDtypeStruct((4, COLS, CH), bf16)
    gathered, last = gather_all(pixels, conv_weight)
    xs, ws, acc, *params = pl.pallas_call(
        early_kernel,
        out_shape=(
            jax.ShapeDtypeStruct((PIX, 8 * CH), bf16),
            jax.ShapeDtypeStruct((9, 8 * CH, CH), bf16),
            jax.ShapeDtypeStruct((3, 6 * COLS, CH), f32),
            jax.ShapeDtypeStruct((1, CH), f32),
            jax.ShapeDtypeStruct((1, CH), f32),
            jax.ShapeDtypeStruct((7, 7, CH), f32),
        ),
        in_specs=[hbm] + [anywhere] * 14 + [hbm] * 3,
        out_specs=(vmem,) * 6,
        scratch_shapes=[pltpu.SemaphoreType.DMA((39,))],
        compiler_params=pltpu.CompilerParams(vmem_limit_bytes=30 << 20),
        cost_estimate=pl.CostEstimate(
            flops=2 * PIX * 9 * EARLY * CH, bytes_accessed=6 << 20, transcendentals=0
        ),
        name="early",
    )(*gathered, conv_bias.reshape(1, CH), depth_bias.reshape(1, CH), depth_weight)
    outer, inner, mid, own = pl.pallas_call(
        late_kernel,
        out_shape=(
            message,
            message,
            jax.ShapeDtypeStruct((2, COLS, CH), bf16),
            jax.ShapeDtypeStruct((4, COLS, CH), f32),
        ),
        in_specs=[vmem, anywhere, vmem, anywhere, vmem],
        out_specs=(vmem,) * 4,
        scratch_shapes=[
            pltpu.VMEM((9, 2 * CH, CH), bf16),
            pltpu.VMEM((3, 6 * COLS, CH), f32),
            pltpu.VMEM((4, COLS, CH), bf16),
            pltpu.VMEM((4, COLS, CH), bf16),
            pltpu.SemaphoreType.DMA((6,)),
        ],
        compiler_params=pltpu.CompilerParams(vmem_limit_bytes=30 << 20),
        cost_estimate=pl.CostEstimate(
            flops=2 * PIX * 9 * 2 * CH * CH, bytes_accessed=4 << 20, transcendentals=0
        ),
        name="late",
    )(xs, ws, acc, last, params[0])
    across = [(i, i + 1) for i in range(1, 31, 2)]
    from_outer = lax.ppermute(outer, "tile", across + [(j, i) for i, j in across])
    from_inner = lax.ppermute(inner, "tile", [(i, i ^ 1) for i in range(32)])
    return pl.pallas_call(
        depth_kernel,
        out_shape=jax.ShapeDtypeStruct((ROWS, COLS, CH), bf16),
        in_specs=[vmem] * 7,
        out_specs=vmem,
        scratch_shapes=[pltpu.VMEM((10, COLS + 16, CH), f32)],
        compiler_params=pltpu.CompilerParams(vmem_limit_bytes=20 << 20),
        cost_estimate=pl.CostEstimate(flops=2 * PIX * 49 * CH, bytes_accessed=2 << 20, transcendentals=0),
        name="depth",
    )(own, mid, from_outer, from_inner, *params)


def solution(mesh):
    in_specs = (
        P("tile", None, "chan"),
        P(None, None, "tile", "chan"),
        P("chan"),
        P(None, None, "chan"),
        P("chan"),
    )
    out_specs = P("tile", None, "chan")
    return jax.shard_map(body, mesh=mesh, in_specs=in_specs, out_specs=out_specs, check_vma=False)
```

```python
import jax
import jax.numpy as jnp
from jax import lax
from jax.experimental import pallas as pl
from jax.experimental.pallas import tpu as pltpu
from jax.sharding import PartitionSpec as P


ROWS, COLS, CH = 4, 256, 128
PIX = ROWS * COLS


def over_a(x):
    return x ^ 1


def over_b(x):
    return (x + 1 if x % 2 else x - 1) % 4


def move(block, partner):
    pairs = []
    for chan in range(8):
        for tile in range(32):
            x, y, hi, z, core = partner(chan // 2, chan % 2, tile // 16, (tile // 2) % 8, tile % 2)
            pairs.append((chan * 32 + tile, (2 * x + y) * 32 + (hi * 8 + z % 8) * 2 + core))
    return lax.ppermute(block, ("chan", "tile"), pairs)


def to_y(x, y, hi, z, core):
    return x, 1 - y, hi, z, core


def to_l(x, y, hi, z, core):
    return (over_b(x) if core else over_a(x)), y, hi, z, core


def to_m(x, y, hi, z, core):
    return (over_a(x) if core else over_b(x)), y, hi, z, core


def to_hi(x, y, hi, z, core):
    return x, y, 1 - hi, z, core


def to_core(x, y, hi, z, core):
    return x, y, hi, z, 1 - core


def to_next(x, y, hi, z, core):
    return x, y, hi, (z - 1 if core else z + 1), core


TAPS = (((0, 0), (0, 1)), ((0, 2), (2, 0)), ((2, 1), (2, 2)), ((1, 0), (1, 1)), ((1, 2),))
EARLY = 6 * CH


def add_taps(pixels, filters, acc):
    for taps in TAPS:
        columns = [filters(3 * a + b) for a, b in taps]
        rhs = jnp.concatenate(columns, axis=1) if len(taps) > 1 else columns[0]
        result = jnp.dot(pixels(), rhs, preferred_element_type=jnp.float32)
        for at, (a, b) in enumerate(taps):
            part = result[:, at * CH : (at + 1) * CH]
            if a == 0:
                acc[b, 512:1536, :] = part
            elif a == 2:
                acc[b, 0:512, :] = part[0:512]
                acc[b, 512:1024, :] += part[512:1024]
            else:
                acc[b, 256:1280, :] += part


class Copies:
    def __init__(self, sems):
        self.sems, self.started = sems, []

    def start(self, src, dst):
        copy = pltpu.make_async_copy(src, dst, self.sems.at[len(self.started)])
        copy.start()
        self.started.append(copy)

    def wait(self):
        for copy in self.started:
            copy.wait()


def block_at(pair, half, z):
    return 2 * ((pair - z // 2 + 5) % 4) + half


def filter_rows(z, at_z, half, at_core, first):
    row = block_at(at_z // 2, half, z) * CH + (at_z % 2) * 64 + at_core * 32 - first
    return pl.ds(pl.multiple_of(row, 32), 32)


def early_kernel(*refs):
    blocks, own_w, other_w, small = refs[:8], refs[8:12], refs[12:15], refs[15:18]
    (xs, ws, acc, *params), sems = refs[18:24], refs[24]
    chan, tile = lax.axis_index("chan"), lax.axis_index("tile")
    x, y = chan // 2, chan % 2
    y_hi, z, core = tile // 16, (tile // 2) % 8, tile % 2
    turn = 1 - 2 * ((x + core) % 2)
    xl, xm, xf = (x + turn + 4) % 4, (x - turn + 4) % 4, (x + 2) % 4
    copies = Copies(sems)
    places = ((x, y), (x, 1 - y), (xl, y), (xm, y), (xl, 1 - y), (xf, y), (xm, 1 - y), (xf, 1 - y))
    for block, (at_x, at_y) in zip(blocks, places):
        index = 2 * at_x + at_y
        at = block_at(index % 4, index // 4, z)
        copies.start(block, xs.at[:, pl.ds(pl.multiple_of(at * CH, CH), CH)])

    def place(array, at_z, at_core):
        for piece in range(array.shape[0] // 9):
            rows = filter_rows(z, at_z, (y_hi + piece // 2) % 2, (at_core + piece) % 2, 0)
            copies.start(array.at[pl.ds(9 * piece, 9)], ws.at[:, rows, :])

    back = 1 - 2 * core
    for steps, array in enumerate(own_w):
        place(array, (z - steps * back + 8) % 8, core)
    for steps, array in enumerate(other_w):
        place(array, (z + (steps + 1) * back + 8) % 8, 1 - core)
    for source, target in zip(small, params):
        copies.start(source, target)
    copies.wait()
    add_taps(lambda: xs[:, 0:EARLY], lambda tap: ws[tap, 0:EARLY, :], acc)


def late_kernel(xs, ws_early, acc_early, last, bias, outer, inner, mid, own, ws, acc, sems):
    tile = lax.axis_index("tile")
    y_hi, z, core = tile // 16, (tile // 2) % 8, tile % 2
    copies = Copies(sems)
    for half in range(2):
        rows = pl.ds(pl.multiple_of(half * CH + (1 - z % 2) * 64, 64), 64)
        early = pl.ds(pl.multiple_of(EARLY + half * CH + (1 - z % 2) * 64, 64), 64)
        copies.start(ws_early.at[:, early, :], ws.at[:, rows, :])
    for piece in range(4):
        rows = filter_rows(z, (z + 4) % 8, (y_hi + piece // 2) % 2, (core + piece) % 2, EARLY)
        copies.start(last.at[pl.ds(9 * piece, 9)], ws.at[:, rows, :])
    copies.wait()
    add_taps(lambda: xs[:, EARLY : 8 * CH], lambda tap: ws[tap], acc)

    column = lax.broadcasted_iota(jnp.int32, (COLS, CH), 0)

    def row_sum(row):
        rows = pl.ds(pl.multiple_of((row + 1 + core * (3 - 2 * row)) * COLS, COLS), COLS)
        total = [acc[b, rows, :] + acc_early[b, rows, :] for b in range(3)]
        left = jnp.where(column == 0, 0.0, pltpu.roll(total[0], 1, 0))
        right = jnp.where(column == COLS - 1, 0.0, pltpu.roll(total[2], COLS - 1, 0))
        return total[1] + left + right

    for slot, row in enumerate((-1, 0, 4, 3)):
        value = row_sum(row)
        own[slot] = value
        if slot < 2:
            outer[slot] = value.astype(jnp.bfloat16)
        else:
            inner[slot - 2] = value.astype(jnp.bfloat16)
    for slot, row in enumerate((1, 2)):
        value = jnp.maximum(row_sum(row) + bias[...], 0.0).astype(jnp.bfloat16)
        mid[slot] = value
        outer[2 + slot] = value
        inner[3 - slot] = value


def add_depth(rows, first, weight, hidden, begin, finish):
    core = lax.axis_index("tile") % 2
    pad = jnp.zeros((len(rows), 8, CH), jnp.float32)
    hidden[:, 0:8, :] = pad
    hidden[:, 264:272, :] = pad
    for at, value in enumerate(rows):
        hidden[at, 8:264, :] = value
    width = 32

    def strip(step, _):
        start = pl.multiple_of(step * width, width)
        sums = [begin(row, pl.ds(start, width)) for row in range(ROWS)]
        for at in range(len(rows)):
            for b in range(7):
                value = hidden[at, pl.ds(start + (5 + b), width), :]
                for row in range(ROWS):
                    a = first + at - row + 3
                    if 0 <= a < 7:
                        sums[row] = sums[row] + value * weight[a + core * (6 - 2 * a), b : b + 1, :]
        for row in range(ROWS):
            finish(row, pl.ds(start, width), sums[row])
        return 0

    lax.fori_loop(0, COLS // width, strip, 0)


def activate(value, bias):
    return jnp.maximum(value + bias[...], 0.0).astype(jnp.bfloat16).astype(jnp.float32)


def depth_early_kernel(own, mid, inner, bias, depth_bias, weight, part, hidden):
    f32 = jnp.float32
    rows = (
        mid[0].astype(f32),
        mid[1].astype(f32),
        activate(own[3] + inner[0].astype(f32), bias),
        activate(inner[1].astype(f32) + own[2], bias),
        inner[2].astype(f32),
        inner[3].astype(f32),
    )

    def finish(row, columns, value):
        part[row, columns, :] = value

    add_depth(
        rows, 1, weight, hidden,
        lambda row, columns: jnp.zeros((columns.size, CH), f32) + depth_bias[...], finish,
    )


def depth_late_kernel(part, own, outer, bias, weight, out, hidden):
    f32 = jnp.float32
    tile = lax.axis_index("tile")
    core = tile % 2
    inside = jnp.logical_and(tile > 0, tile < 31).astype(f32)
    rows = (
        outer[3].astype(f32) * inside,
        outer[2].astype(f32) * inside,
        activate(outer[1].astype(f32) + own[0], bias) * inside,
        activate(own[1] + outer[0].astype(f32), bias),
    )

    def finish(row, columns, value):
        out[row + core * (3 - 2 * row), columns, :] = value.astype(jnp.bfloat16)

    add_depth(rows, -3, weight, hidden, lambda row, columns: part[row, columns, :], finish)


def gather_all(pixels, weight):
    p0 = pixels.reshape(PIX, CH)
    w0 = weight.reshape(9, 32, CH)
    h0 = move(w0, to_hi)
    w0_other = move(w0, to_core)
    p_y, p_l, p_m = move(p0, to_y), move(p0, to_l), move(p0, to_m)
    w0 = jnp.concatenate([w0, w0_other, h0, move(h0, to_core)])
    w1 = move(w0, to_next)
    w2 = move(w1, to_next)
    o1 = move(w1, to_core)
    p_ly, p_ml, p_ym = move(p_l, to_y), move(p_m, to_l), move(p_y, to_m)
    w3 = move(w2, to_next)
    o2 = move(w2, to_core)
    p_far = move(p_ym, to_l)
    w4 = move(w3, to_next)
    o3 = move(w3, to_core)
    return (in_hbm(p0), p_y, p_l, p_m, p_ly, p_ml, p_ym, p_far, w0, w1, w2, w3, o1, o2, o3), w4


def in_hbm(array):
    return pltpu.with_memory_space_constraint(array, pltpu.HBM)


def body(pixels, conv_weight, conv_bias, depth_weight, depth_bias):
    anywhere, vmem = pl.BlockSpec(memory_space=pl.ANY), pl.BlockSpec(memory_space=pltpu.VMEM)
    hbm = pl.BlockSpec(memory_space=pltpu.HBM)
    f32, bf16 = jnp.float32, jnp.bfloat16
    message = jax.ShapeDtypeStruct((4, COLS, CH), bf16)
    gathered, last = gather_all(pixels, conv_weight)
    xs, ws, acc, *params = pl.pallas_call(
        early_kernel,
        out_shape=(
            jax.ShapeDtypeStruct((PIX, 8 * CH), bf16),
            jax.ShapeDtypeStruct((9, 8 * CH, CH), bf16),
            jax.ShapeDtypeStruct((3, 6 * COLS, CH), f32),
            jax.ShapeDtypeStruct((1, CH), f32),
            jax.ShapeDtypeStruct((1, CH), f32),
            jax.ShapeDtypeStruct((7, 7, CH), f32),
        ),
        in_specs=[hbm] + [anywhere] * 14 + [hbm] * 3,
        out_specs=(vmem,) * 6,
        scratch_shapes=[pltpu.SemaphoreType.DMA((39,))],
        compiler_params=pltpu.CompilerParams(vmem_limit_bytes=30 << 20),
        cost_estimate=pl.CostEstimate(
            flops=2 * PIX * 9 * EARLY * CH, bytes_accessed=6 << 20, transcendentals=0
        ),
        name="early",
    )(
        *gathered,
        in_hbm(conv_bias.reshape(1, CH)),
        in_hbm(depth_bias.reshape(1, CH)),
        in_hbm(depth_weight),
    )
    outer, inner, mid, own = pl.pallas_call(
        late_kernel,
        out_shape=(
            message,
            message,
            jax.ShapeDtypeStruct((2, COLS, CH), bf16),
            jax.ShapeDtypeStruct((4, COLS, CH), f32),
        ),
        in_specs=[vmem, anywhere, vmem, anywhere, vmem],
        out_specs=(vmem,) * 4,
        scratch_shapes=[
            pltpu.VMEM((9, 2 * CH, CH), bf16),
            pltpu.VMEM((3, 6 * COLS, CH), f32),
            pltpu.SemaphoreType.DMA((6,)),
        ],
        compiler_params=pltpu.CompilerParams(vmem_limit_bytes=30 << 20),
        cost_estimate=pl.CostEstimate(
            flops=2 * PIX * 9 * 2 * CH * CH, bytes_accessed=4 << 20, transcendentals=0
        ),
        name="late",
    )(xs, ws, acc, last, params[0])
    bias, depth_bias, weight = params
    across = [(i, i + 1) for i in range(1, 31, 2)]
    from_outer = lax.ppermute(outer, "tile", across + [(j, i) for i, j in across])
    from_inner = lax.ppermute(inner, "tile", [(i, i ^ 1) for i in range(32)])
    part = depth(depth_early_kernel, f32, 6, own, mid, from_inner, bias, depth_bias, weight)
    return depth(depth_late_kernel, bf16, 4, part, own, from_outer, bias, weight)


def depth(kernel, dtype, rows, *operands):
    vmem = pl.BlockSpec(memory_space=pltpu.VMEM)
    return pl.pallas_call(
        kernel,
        out_shape=jax.ShapeDtypeStruct((ROWS, COLS, CH), dtype),
        in_specs=[vmem] * len(operands),
        out_specs=vmem,
        scratch_shapes=[pltpu.VMEM((rows, COLS + 16, CH), jnp.float32)],
        compiler_params=pltpu.CompilerParams(vmem_limit_bytes=20 << 20),
        cost_estimate=pl.CostEstimate(flops=5 * rows * COLS * 49 * CH, bytes_accessed=2 << 20, transcendentals=0),
        name="depth",
    )(*operands)


def solution(mesh):
    in_specs = (
        P("tile", None, "chan"),
        P(None, None, "tile", "chan"),
        P("chan"),
        P(None, None, "chan"),
        P("chan"),
    )
    out_specs = P("tile", None, "chan")
    return jax.shard_map(body, mesh=mesh, in_specs=in_specs, out_specs=out_specs, check_vma=False)
```

```python
import jax
import jax.numpy as jnp
from jax import lax
from jax.experimental import pallas as pl
from jax.experimental.pallas import tpu as pltpu
from jax.sharding import PartitionSpec as P


ROWS, COLS, CH = 4, 256, 128
PIX = ROWS * COLS


def over_a(x):
    return x ^ 1


def over_b(x):
    return (x + 1 if x % 2 else x - 1) % 4


def move(block, partner):
    pairs = []
    for chan in range(8):
        for tile in range(32):
            x, y, hi, z, core = partner(chan // 2, chan % 2, tile // 16, (tile // 2) % 8, tile % 2)
            pairs.append((chan * 32 + tile, (2 * x + y) * 32 + (hi * 8 + z % 8) * 2 + core))
    return lax.ppermute(block, ("chan", "tile"), pairs)


def to_y(x, y, hi, z, core):
    return x, 1 - y, hi, z, core


def to_l(x, y, hi, z, core):
    return (over_b(x) if core else over_a(x)), y, hi, z, core


def to_m(x, y, hi, z, core):
    return (over_a(x) if core else over_b(x)), y, hi, z, core


def to_hi(x, y, hi, z, core):
    return x, y, 1 - hi, z, core


def to_core(x, y, hi, z, core):
    return x, y, hi, z, 1 - core


def to_next(x, y, hi, z, core):
    return x, y, hi, (z - 1 if core else z + 1), core


TAPS = (((0, 0), (0, 1)), ((0, 2), (2, 0)), ((2, 1), (2, 2)), ((1, 0), (1, 1)), ((1, 2),))


def add_taps(pixels, filters, acc, base=None):
    def put(b, begin, value, add):
        rows = slice(begin, begin + value.shape[0])
        before = acc if add else base
        acc[b, rows, :] = value if before is None else before[b, rows, :] + value

    for taps in TAPS:
        columns = [filters[3 * a + b] for a, b in taps]
        rhs = jnp.concatenate(columns, axis=1) if len(taps) > 1 else columns[0]
        result = jnp.dot(pixels(), rhs, preferred_element_type=jnp.float32)
        for at, (a, b) in enumerate(taps):
            part = result[:, at * CH : (at + 1) * CH]
            if a == 0:
                put(b, 512, part, False)
            elif a == 2:
                put(b, 0, part[0:512], False)
                put(b, 512, part[512:1024], True)
            else:
                put(b, 256, part, True)


class Copies:
    def __init__(self, sems):
        self.sems, self.started = sems, []

    def start(self, src, dst):
        copy = pltpu.make_async_copy(src, dst, self.sems.at[len(self.started)])
        copy.start()
        self.started.append(copy)

    def wait(self):
        for copy in self.started:
            copy.wait()


def pair_at(pair, z):
    ahead = ((pair - z // 2) * (1 - 2 * (z % 2)) + 8) % 4
    return (ahead % 3 + 1) * ((ahead + 3) // 4)


class Filters:
    def __init__(self, copies, target):
        self.copies, self.target = copies, target
        tile = lax.axis_index("tile")
        self.y_hi, self.z, self.core = tile // 16, (tile // 2) % 8, tile % 2
        self.partner_back = (self.core + self.z) % 2 == 1

    def each_piece(self, array, odd, first, core):
        for piece in range(4):
            half, at_core = (self.y_hi + piece // 2) % 2, (core + piece) % 2
            source, at = (array[piece // 2], piece % 2) if isinstance(array, tuple) else (array, piece)
            row = first + half * CH + odd * 64 + at_core * 32
            rows = pl.ds(pl.multiple_of(row, 32), 32)
            yield source.at[pl.ds(9 * at, 9)], self.target.at[:, rows, :]

    def place(self, array, odd, first, core):
        for src, dst in self.each_piece(array, odd, first, core):
            self.copies.start(src, dst)

    def place_one(self, mine, others, towards_partner, odd, first):
        use_mine = self.partner_back == towards_partner
        sems = [self.copies.sems.at[len(self.copies.started) + piece] for piece in range(4)]

        def start(array, core):
            for (src, dst), sem in zip(self.each_piece(array, odd, first, core), sems):
                pltpu.make_async_copy(src, dst, sem).start()

        pl.when(use_mine)(lambda: start(mine, self.core))
        pl.when(jnp.logical_not(use_mine))(lambda: start(others, 1 - self.core))
        for sem in sems:
            same_size = pltpu.make_async_copy(mine[0].at[pl.ds(0, 9)], self.target.at[:, pl.ds(0, 32), :], sem)
            self.copies.started.append(same_size)


def first_kernel(*refs):
    blocks, w0, w1, w2, (o1, o2), small = refs[:8], refs[8:10], refs[10:12], refs[12:14], refs[14:16], refs[16:19]
    (xs, acc, *params), (ws, sems) = refs[19:24], refs[24:]
    chan = lax.axis_index("chan")
    x, y = chan // 2, chan % 2
    copies = Copies(sems)
    filters = Filters(copies, ws)
    z, core = filters.z, filters.core
    turn = 1 - 2 * ((x + core) % 2)
    xl, xm, xf = (x + turn + 4) % 4, (x - turn + 4) % 4, (x + 2) % 4
    places = ((x, y), (x, 1 - y), (xl, y), (xm, y), (xl, 1 - y), (xf, y), (xm, 1 - y), (xf, 1 - y))
    for block, (at_x, at_y) in zip(blocks, places):
        index = 2 * at_x + at_y
        at = 2 * pair_at(index % 4, z) + index // 4
        copies.start(block, xs.at[:, pl.ds(pl.multiple_of(at * CH, CH), CH)])
    even, odd = z % 2, 1 - z % 2
    filters.place(w0, even, 0, core)
    filters.place_one(w1, o1, True, odd, 0)
    filters.place_one(w1, o1, False, odd, 2 * CH)
    filters.place_one(w2, o2, False, even, 2 * CH)
    for source, target in zip(small, params):
        copies.start(source, target)
    copies.wait()
    add_taps(lambda: xs[:, 0 : 4 * CH], ws, acc)


def second_kernel(xs, base, a2, g2, a3, g3, o2, o3, acc, ws, sems):
    w2, w3 = (a2, g2), (a3, g3)
    copies = Copies(sems)
    filters = Filters(copies, ws)
    even, odd = filters.z % 2, 1 - filters.z % 2
    filters.place_one(w2, o2, True, even, 0)
    filters.place_one(w3, o3, True, odd, 0)
    copies.wait()
    add_taps(lambda: xs[:, 4 * CH : 6 * CH], ws, acc, base)


def third_kernel(xs, base, a3, g3, o3, a4, g4, bias, outer, inner, mid, own, ws, acc, sems):
    w3, w4 = (a3, g3), (a4, g4)
    copies = Copies(sems)
    filters = Filters(copies, ws)
    core, even, odd = filters.core, filters.z % 2, 1 - filters.z % 2
    filters.place_one(w3, o3, False, odd, 0)
    filters.place(w4, even, 0, core)
    copies.wait()
    add_taps(lambda: xs[:, 6 * CH : 8 * CH], ws, acc, base)

    column = lax.broadcasted_iota(jnp.int32, (COLS, CH), 0)

    def row_sum(row):
        rows = pl.ds(pl.multiple_of((row + 1 + core * (3 - 2 * row)) * COLS, COLS), COLS)
        total = [acc[b, rows, :] for b in range(3)]
        left = jnp.where(column == 0, 0.0, pltpu.roll(total[0], 1, 0))
        right = jnp.where(column == COLS - 1, 0.0, pltpu.roll(total[2], COLS - 1, 0))
        return total[1] + left + right

    for slot, row in enumerate((-1, 0, 4, 3)):
        value = row_sum(row)
        own[slot] = value
        if slot < 2:
            outer[slot] = value.astype(jnp.bfloat16)
        else:
            inner[slot - 2] = value.astype(jnp.bfloat16)
    for slot, row in enumerate((1, 2)):
        value = jnp.maximum(row_sum(row) + bias[...], 0.0).astype(jnp.bfloat16)
        mid[slot] = value
        outer[2 + slot] = value
        inner[3 - slot] = value


def add_depth(rows, first, weight, hidden, begin, finish):
    core = lax.axis_index("tile") % 2
    pad = jnp.zeros((len(rows), 8, CH), jnp.float32)
    hidden[:, 0:8, :] = pad
    hidden[:, 264:272, :] = pad
    for at, value in enumerate(rows):
        hidden[at, 8:264, :] = value
    width = 32

    def strip(step, _):
        start = pl.multiple_of(step * width, width)
        sums = [begin(row, pl.ds(start, width)) for row in range(ROWS)]
        for at in range(len(rows)):
            for b in range(7):
                value = hidden[at, pl.ds(start + (5 + b), width), :]
                for row in range(ROWS):
                    a = first + at - row + 3
                    if 0 <= a < 7:
                        sums[row] = sums[row] + value * weight[a + core * (6 - 2 * a), b : b + 1, :]
        for row in range(ROWS):
            finish(row, pl.ds(start, width), sums[row])
        return 0

    lax.fori_loop(0, COLS // width, strip, 0)


def activate(value, bias):
    return jnp.maximum(value + bias[...], 0.0).astype(jnp.bfloat16).astype(jnp.float32)


def depth_early_kernel(own, mid, inner, bias, depth_bias, weight, part, hidden):
    f32 = jnp.float32
    rows = (
        mid[0].astype(f32),
        mid[1].astype(f32),
        activate(own[3] + inner[0].astype(f32), bias),
        activate(inner[1].astype(f32) + own[2], bias),
        inner[2].astype(f32),
        inner[3].astype(f32),
    )

    def finish(row, columns, value):
        part[row, columns, :] = value

    add_depth(
        rows, 1, weight, hidden,
        lambda row, columns: jnp.zeros((columns.size, CH), f32) + depth_bias[...], finish,
    )


def depth_late_kernel(part, own, outer, bias, weight, out, hidden):
    f32 = jnp.float32
    tile = lax.axis_index("tile")
    core = tile % 2
    inside = jnp.logical_and(tile > 0, tile < 31).astype(f32)
    rows = (
        outer[3].astype(f32) * inside,
        outer[2].astype(f32) * inside,
        activate(outer[1].astype(f32) + own[0], bias) * inside,
        activate(own[1] + outer[0].astype(f32), bias),
    )

    def finish(row, columns, value):
        out[row + core * (3 - 2 * row), columns, :] = value.astype(jnp.bfloat16)

    add_depth(rows, -3, weight, hidden, lambda row, columns: part[row, columns, :], finish)


def gather_all(pixels, weight):
    p0 = pixels.reshape(PIX, CH)
    w0 = weight.reshape(9, 32, CH)
    h0 = move(w0, to_hi)
    w0_other = move(w0, to_core)
    p_y, p_l, p_m = move(p0, to_y), move(p0, to_l), move(p0, to_m)
    a0 = jnp.concatenate([w0, w0_other])
    a1 = move(a0, to_next)
    g0 = jnp.concatenate([h0, move(h0, to_core)])
    g1 = move(g0, to_next)
    a2, g2 = move(a1, to_next), move(g1, to_next)
    both = jnp.concatenate([a1, g1])
    o1 = move(both, to_core)
    p_ly, p_ml, p_ym = move(p_l, to_y), move(p_m, to_l), move(p_y, to_m)
    a3, g3 = move(a2, to_next), move(g2, to_next)
    both = jnp.concatenate([a2, g2])
    o2 = move(both, to_core)
    p_far = move(p_ym, to_l)
    a4, g4 = move(a3, to_next), move(g3, to_next)
    both = jnp.concatenate([a3, g3])
    o3 = move(both, to_core)
    blocks = (in_hbm(p0), p_y, p_l, p_m, p_ly, p_ml, p_ym, p_far)
    return blocks, ((a0, g0), (a1, g1), (a2, g2), (a3, g3), (a4, g4)), (o1, o2, o3)


def in_hbm(array):
    return pltpu.with_memory_space_constraint(array, pltpu.HBM)


def body(pixels, conv_weight, conv_bias, depth_weight, depth_bias):
    anywhere, vmem = pl.BlockSpec(memory_space=pl.ANY), pl.BlockSpec(memory_space=pltpu.VMEM)
    hbm = pl.BlockSpec(memory_space=pltpu.HBM)
    f32, bf16 = jnp.float32, jnp.bfloat16
    message = jax.ShapeDtypeStruct((4, COLS, CH), bf16)
    sums = jax.ShapeDtypeStruct((3, 6 * COLS, CH), f32)

    def settings(blocks):
        return dict(
            compiler_params=pltpu.CompilerParams(vmem_limit_bytes=30 << 20),
            cost_estimate=pl.CostEstimate(
                flops=2 * PIX * 9 * blocks * CH * CH, bytes_accessed=4 << 20, transcendentals=0
            ),
        )

    blocks, (w0, w1, w2, w3, w4), (o1, o2, o3) = gather_all(pixels, conv_weight)
    xs, acc, *params = pl.pallas_call(
        first_kernel,
        out_shape=(
            jax.ShapeDtypeStruct((PIX, 8 * CH), bf16),
            sums,
            jax.ShapeDtypeStruct((1, CH), f32),
            jax.ShapeDtypeStruct((1, CH), f32),
            jax.ShapeDtypeStruct((7, 7, CH), f32),
        ),
        in_specs=[hbm] + [anywhere] * 15 + [hbm] * 3,
        out_specs=(vmem,) * 5,
        scratch_shapes=[pltpu.VMEM((9, 4 * CH, CH), bf16), pltpu.SemaphoreType.DMA((27,))],
        name="first",
        **settings(4),
    )(
        *blocks, *w0, *w1, *w2, o1, o2,
        in_hbm(conv_bias.reshape(1, CH)),
        in_hbm(depth_bias.reshape(1, CH)),
        in_hbm(depth_weight),
    )
    acc = pl.pallas_call(
        second_kernel,
        out_shape=sums,
        in_specs=[vmem] * 2 + [anywhere] * 6,
        out_specs=vmem,
        scratch_shapes=[pltpu.VMEM((9, 2 * CH, CH), bf16), pltpu.SemaphoreType.DMA((8,))],
        name="second",
        **settings(2),
    )(xs, acc, *w2, *w3, o2, o3)
    outer, inner, mid, own = pl.pallas_call(
        third_kernel,
        out_shape=(
            message,
            message,
            jax.ShapeDtypeStruct((2, COLS, CH), bf16),
            jax.ShapeDtypeStruct((4, COLS, CH), f32),
        ),
        in_specs=[vmem] * 2 + [anywhere] * 5 + [vmem],
        out_specs=(vmem,) * 4,
        scratch_shapes=[
            pltpu.VMEM((9, 2 * CH, CH), bf16),
            pltpu.VMEM((3, 6 * COLS, CH), f32),
            pltpu.SemaphoreType.DMA((8,)),
        ],
        name="third",
        **settings(2),
    )(xs, acc, *w3, o3, *w4, params[0])
    bias, depth_bias, weight = params
    across = [(i, i + 1) for i in range(1, 31, 2)]
    from_outer = lax.ppermute(outer, "tile", across + [(j, i) for i, j in across])
    from_inner = lax.ppermute(inner, "tile", [(i, i ^ 1) for i in range(32)])
    part = depth(depth_early_kernel, f32, 6, own, mid, from_inner, bias, depth_bias, weight)
    return depth(depth_late_kernel, bf16, 4, part, own, from_outer, bias, weight)


def depth(kernel, dtype, rows, *operands):
    vmem = pl.BlockSpec(memory_space=pltpu.VMEM)
    return pl.pallas_call(
        kernel,
        out_shape=jax.ShapeDtypeStruct((ROWS, COLS, CH), dtype),
        in_specs=[vmem] * len(operands),
        out_specs=vmem,
        scratch_shapes=[pltpu.VMEM((rows, COLS + 16, CH), jnp.float32)],
        compiler_params=pltpu.CompilerParams(vmem_limit_bytes=20 << 20),
        cost_estimate=pl.CostEstimate(flops=5 * rows * COLS * 49 * CH, bytes_accessed=2 << 20, transcendentals=0),
        name="depth",
    )(*operands)


def solution(mesh):
    in_specs = (
        P("tile", None, "chan"),
        P(None, None, "tile", "chan"),
        P("chan"),
        P(None, None, "chan"),
        P("chan"),
    )
    out_specs = P("tile", None, "chan")
    return jax.shard_map(body, mesh=mesh, in_specs=in_specs, out_specs=out_specs, check_vma=False)
```

```python
import jax
import jax.numpy as jnp
from jax import lax
from jax.experimental import pallas as pl
from jax.experimental.pallas import tpu as pltpu
from jax.sharding import PartitionSpec as P


ROWS, COLS, CH = 4, 256, 128
PIX = ROWS * COLS


def over_a(x):
    return x ^ 1


def over_b(x):
    return (x + 1 if x % 2 else x - 1) % 4


def move(block, partner):
    pairs = []
    for chan in range(8):
        for tile in range(32):
            x, y, hi, z, core = partner(chan // 2, chan % 2, tile // 16, (tile // 2) % 8, tile % 2)
            pairs.append((chan * 32 + tile, (2 * x + y) * 32 + (hi * 8 + z % 8) * 2 + core))
    return lax.ppermute(block, ("chan", "tile"), pairs)


def to_y(x, y, hi, z, core):
    return x, 1 - y, hi, z, core


def to_l(x, y, hi, z, core):
    return (over_b(x) if core else over_a(x)), y, hi, z, core


def to_m(x, y, hi, z, core):
    return (over_a(x) if core else over_b(x)), y, hi, z, core


def to_hi(x, y, hi, z, core):
    return x, y, 1 - hi, z, core


def to_core(x, y, hi, z, core):
    return x, y, hi, z, 1 - core


def to_next(x, y, hi, z, core):
    return x, y, hi, (z - 1 if core else z + 1), core


TAPS = (((0, 0), (0, 1)), ((0, 2), (2, 0)), ((2, 1), (2, 2)), ((1, 0), (1, 1)), ((1, 2),))


def add_taps(pixels, filters, acc, base=None):
    def put(b, begin, value, add):
        rows = slice(begin, begin + value.shape[0])
        before = acc if add else base
        acc[b, rows, :] = value if before is None else before[b, rows, :] + value

    for taps in TAPS:
        columns = [filters[3 * a + b] for a, b in taps]
        rhs = jnp.concatenate(columns, axis=1) if len(taps) > 1 else columns[0]
        result = jnp.dot(pixels(), rhs, preferred_element_type=jnp.float32)
        for at, (a, b) in enumerate(taps):
            part = result[:, at * CH : (at + 1) * CH]
            if a == 0:
                put(b, 512, part, False)
            elif a == 2:
                put(b, 0, part[0:512], False)
                put(b, 512, part[512:1024], True)
            else:
                put(b, 256, part, True)


class Copies:
    def __init__(self, sems):
        self.sems, self.started = sems, []

    def start(self, src, dst):
        copy = pltpu.make_async_copy(src, dst, self.sems.at[len(self.started)])
        copy.start()
        self.started.append(copy)

    def wait(self):
        for copy in self.started:
            copy.wait()


def pair_at(pair, z):
    ahead = ((pair - z // 2) * (1 - 2 * (z % 2)) + 8) % 4
    return (ahead % 3 + 1) * ((ahead + 3) // 4)


class Filters:
    def __init__(self, target):
        self.target = target
        tile = lax.axis_index("tile")
        self.y_hi, self.z, self.core = tile // 16, (tile // 2) % 8, tile % 2
        self.partner_back = (self.core + self.z) % 2 == 1

    def place(self, arrays, odd, first, core):
        for piece in range(4):
            half, at_core = (self.y_hi + piece // 2) % 2, (core + piece) % 2
            row = first + half * CH + odd * 64 + at_core * 32
            rows = pl.ds(pl.multiple_of(row, 32), 32)
            array, offset = arrays[piece // 2]
            begin = offset + 9 * (piece % 2)
            self.target[:, rows, :] = array[begin : begin + 9]

    def place_one(self, mine, others, towards_partner, odd, first):
        use_mine = self.partner_back == towards_partner
        pl.when(use_mine)(lambda: self.place(mine, odd, first, self.core))
        pl.when(jnp.logical_not(use_mine))(lambda: self.place(others, odd, first, 1 - self.core))


def rows_of(first, second, at=0):
    return (first, at), (second, at)


def of_pack(pack, slot):
    return (pack, 36 * slot), (pack, 36 * slot + 18)


def first_kernel(*refs):
    blocks, (a0, g0, a1, g1, a2, g2, o12), small = refs[:8], refs[8:15], refs[15:18]
    (xs, acc, *params), (ws, sems) = refs[18:23], refs[23:]
    chan = lax.axis_index("chan")
    x, y = chan // 2, chan % 2
    copies = Copies(sems)
    filters = Filters(ws)
    z, core = filters.z, filters.core
    turn = 1 - 2 * ((x + core) % 2)
    xl, xm, xf = (x + turn + 4) % 4, (x - turn + 4) % 4, (x + 2) % 4
    places = ((x, y), (x, 1 - y), (xl, y), (xm, y), (xl, 1 - y), (xf, y), (xm, 1 - y), (xf, 1 - y))
    for block, (at_x, at_y) in zip(blocks, places):
        index = 2 * at_x + at_y
        at = 2 * pair_at(index % 4, z) + index // 4
        columns = pl.ds(pl.multiple_of(at * CH, CH), CH)
        if block is blocks[0]:
            copies.start(block, xs.at[:, columns])
            for source, target in zip(small, params):
                copies.start(source, target)
        else:
            xs[:, columns] = block[...]
    even, odd = z % 2, 1 - z % 2
    filters.place(rows_of(a0, g0), even, 0, core)
    filters.place_one(rows_of(a1, g1), of_pack(o12, 0), True, odd, 0)
    filters.place_one(rows_of(a1, g1), of_pack(o12, 0), False, odd, 2 * CH)
    filters.place_one(rows_of(a2, g2), of_pack(o12, 1), False, even, 2 * CH)
    copies.wait()
    add_taps(lambda: xs[:, 0 : 4 * CH], ws, acc)


def second_kernel(xs, base, a2, g2, a3, g3, o12, o3, acc, ws):
    filters = Filters(ws)
    even, odd = filters.z % 2, 1 - filters.z % 2
    filters.place_one(rows_of(a2, g2), of_pack(o12, 1), True, even, 0)
    filters.place_one(rows_of(a3, g3), of_pack(o3, 0), True, odd, 0)
    add_taps(lambda: xs[:, 4 * CH : 6 * CH], ws, acc, base)


def third_kernel(xs, base, a3, g3, o3, a4, g4, bias, outer, inner, mid, own, ws, acc):
    filters = Filters(ws)
    core, even, odd = filters.core, filters.z % 2, 1 - filters.z % 2
    filters.place_one(rows_of(a3, g3), of_pack(o3, 0), False, odd, 0)
    filters.place(rows_of(a4, g4), even, 0, core)
    add_taps(lambda: xs[:, 6 * CH : 8 * CH], ws, acc, base)

    column = lax.broadcasted_iota(jnp.int32, (COLS, CH), 0)

    def row_sum(row):
        rows = pl.ds(pl.multiple_of((row + 1 + core * (3 - 2 * row)) * COLS, COLS), COLS)
        total = [acc[b, rows, :] for b in range(3)]
        left = jnp.where(column == 0, 0.0, pltpu.roll(total[0], 1, 0))
        right = jnp.where(column == COLS - 1, 0.0, pltpu.roll(total[2], COLS - 1, 0))
        return total[1] + left + right

    for slot, row in enumerate((-1, 0, 4, 3)):
        value = row_sum(row)
        own[slot] = value
        if slot < 2:
            outer[slot] = value.astype(jnp.bfloat16)
        else:
            inner[slot - 2] = value.astype(jnp.bfloat16)
    for slot, row in enumerate((1, 2)):
        value = jnp.maximum(row_sum(row) + bias[...], 0.0).astype(jnp.bfloat16)
        mid[slot] = value
        outer[2 + slot] = value
        inner[3 - slot] = value


def add_depth(rows, first, weight, hidden, begin, finish):
    core = lax.axis_index("tile") % 2
    pad = jnp.zeros((len(rows), 8, CH), jnp.float32)
    hidden[:, 0:8, :] = pad
    hidden[:, 264:272, :] = pad
    for at, value in enumerate(rows):
        hidden[at, 8:264, :] = value
    width = 32

    def strip(step, _):
        start = pl.multiple_of(step * width, width)
        sums = [begin(row, pl.ds(start, width)) for row in range(ROWS)]
        for at in range(len(rows)):
            for b in range(7):
                value = hidden[at, pl.ds(start + (5 + b), width), :]
                for row in range(ROWS):
                    a = first + at - row + 3
                    if 0 <= a < 7:
                        sums[row] = sums[row] + value * weight[a + core * (6 - 2 * a), b : b + 1, :]
        for row in range(ROWS):
            finish(row, pl.ds(start, width), sums[row])
        return 0

    lax.fori_loop(0, COLS // width, strip, 0)


def activate(value, bias):
    return jnp.maximum(value + bias[...], 0.0).astype(jnp.bfloat16).astype(jnp.float32)


def depth_early_kernel(own, mid, inner, bias, depth_bias, weight, part, hidden):
    f32 = jnp.float32
    rows = (
        mid[0].astype(f32),
        mid[1].astype(f32),
        activate(own[3] + inner[0].astype(f32), bias),
        activate(inner[1].astype(f32) + own[2], bias),
        inner[2].astype(f32),
        inner[3].astype(f32),
    )

    def finish(row, columns, value):
        part[row, columns, :] = value

    add_depth(
        rows, 1, weight, hidden,
        lambda row, columns: jnp.zeros((columns.size, CH), f32) + depth_bias[...], finish,
    )


def depth_late_kernel(part, own, outer, bias, weight, out, hidden):
    f32 = jnp.float32
    tile = lax.axis_index("tile")
    core = tile % 2
    inside = jnp.logical_and(tile > 0, tile < 31).astype(f32)
    rows = (
        outer[3].astype(f32) * inside,
        outer[2].astype(f32) * inside,
        activate(outer[1].astype(f32) + own[0], bias) * inside,
        activate(own[1] + outer[0].astype(f32), bias),
    )

    def finish(row, columns, value):
        out[row + core * (3 - 2 * row), columns, :] = value.astype(jnp.bfloat16)

    add_depth(rows, -3, weight, hidden, lambda row, columns: part[row, columns, :], finish)


def gather_all(pixels, weight):
    p0 = pixels.reshape(PIX, CH)
    w0 = weight.reshape(9, 32, CH)
    h0 = move(w0, to_hi)
    w0_other = move(w0, to_core)
    p_y, p_l, p_m = move(p0, to_y), move(p0, to_l), move(p0, to_m)
    a0 = jnp.concatenate([w0, w0_other])
    a1 = move(a0, to_next)
    g0 = jnp.concatenate([h0, move(h0, to_core)])
    g1 = move(g0, to_next)
    a2, g2 = move(a1, to_next), move(g1, to_next)
    p_ly, p_ml, p_ym = move(p_l, to_y), move(p_m, to_l), move(p_y, to_m)
    a3, g3 = move(a2, to_next), move(g2, to_next)
    both = jnp.concatenate([a1, g1, a2, g2])
    o12 = move(both, to_core)
    p_far = move(p_ym, to_l)
    a4, g4 = move(a3, to_next), move(g3, to_next)
    both = jnp.concatenate([a3, g3])
    o3 = move(both, to_core)
    blocks = (in_hbm(p0), p_y, p_l, p_m, p_ly, p_ml, p_ym, p_far)
    return blocks, (a0, g0, a1, g1, a2, g2, a3, g3, a4, g4), o12, o3


def in_hbm(array):
    return pltpu.with_memory_space_constraint(array, pltpu.HBM)


def body(pixels, conv_weight, conv_bias, depth_weight, depth_bias):
    vmem = pl.BlockSpec(memory_space=pltpu.VMEM)
    hbm = pl.BlockSpec(memory_space=pltpu.HBM)
    f32, bf16 = jnp.float32, jnp.bfloat16
    message = jax.ShapeDtypeStruct((4, COLS, CH), bf16)
    sums = jax.ShapeDtypeStruct((3, 6 * COLS, CH), f32)

    def settings(blocks):
        return dict(
            compiler_params=pltpu.CompilerParams(vmem_limit_bytes=30 << 20),
            cost_estimate=pl.CostEstimate(
                flops=2 * PIX * 9 * blocks * CH * CH, bytes_accessed=4 << 20, transcendentals=0
            ),
        )

    blocks, filters, o12, o3 = gather_all(pixels, conv_weight)
    xs, acc, *params = pl.pallas_call(
        first_kernel,
        out_shape=(
            jax.ShapeDtypeStruct((PIX, 8 * CH), bf16),
            sums,
            jax.ShapeDtypeStruct((1, CH), f32),
            jax.ShapeDtypeStruct((1, CH), f32),
            jax.ShapeDtypeStruct((7, 7, CH), f32),
        ),
        in_specs=[hbm] + [vmem] * 14 + [hbm] * 3,
        out_specs=(vmem,) * 5,
        scratch_shapes=[pltpu.VMEM((9, 4 * CH, CH), bf16), pltpu.SemaphoreType.DMA((4,))],
        name="first",
        **settings(4),
    )(
        *blocks, *filters[:6], o12,
        in_hbm(conv_bias.reshape(1, CH)),
        in_hbm(depth_bias.reshape(1, CH)),
        in_hbm(depth_weight),
    )
    acc = pl.pallas_call(
        second_kernel,
        out_shape=sums,
        in_specs=[vmem] * 8,
        out_specs=vmem,
        scratch_shapes=[pltpu.VMEM((9, 2 * CH, CH), bf16)],
        name="second",
        **settings(2),
    )(xs, acc, *filters[4:8], o12, o3)
    outer, inner, mid, own = pl.pallas_call(
        third_kernel,
        out_shape=(
            message,
            message,
            jax.ShapeDtypeStruct((2, COLS, CH), bf16),
            jax.ShapeDtypeStruct((4, COLS, CH), f32),
        ),
        in_specs=[vmem] * 8,
        out_specs=(vmem,) * 4,
        scratch_shapes=[
            pltpu.VMEM((9, 2 * CH, CH), bf16),
            pltpu.VMEM((3, 6 * COLS, CH), f32),
        ],
        name="third",
        **settings(2),
    )(xs, acc, *filters[6:8], o3, *filters[8:], params[0])
    bias, depth_bias, weight = params
    across = [(i, i + 1) for i in range(1, 31, 2)]
    from_outer = lax.ppermute(outer, "tile", across + [(j, i) for i, j in across])
    from_inner = lax.ppermute(inner, "tile", [(i, i ^ 1) for i in range(32)])
    part = depth(depth_early_kernel, f32, 6, own, mid, from_inner, bias, depth_bias, weight)
    return depth(depth_late_kernel, bf16, 4, part, own, from_outer, bias, weight)


def depth(kernel, dtype, rows, *operands):
    vmem = pl.BlockSpec(memory_space=pltpu.VMEM)
    return pl.pallas_call(
        kernel,
        out_shape=jax.ShapeDtypeStruct((ROWS, COLS, CH), dtype),
        in_specs=[vmem] * len(operands),
        out_specs=vmem,
        scratch_shapes=[pltpu.VMEM((rows, COLS + 16, CH), jnp.float32)],
        compiler_params=pltpu.CompilerParams(vmem_limit_bytes=20 << 20),
        cost_estimate=pl.CostEstimate(flops=5 * rows * COLS * 49 * CH, bytes_accessed=2 << 20, transcendentals=0),
        name="depth",
    )(*operands)


def solution(mesh):
    in_specs = (
        P("tile", None, "chan"),
        P(None, None, "tile", "chan"),
        P("chan"),
        P(None, None, "chan"),
        P("chan"),
    )
    out_specs = P("tile", None, "chan")
    return jax.shard_map(body, mesh=mesh, in_specs=in_specs, out_specs=out_specs, check_vma=False)
```

```python
import jax
import jax.numpy as jnp
from jax import lax
from jax.experimental import pallas as pl
from jax.experimental.pallas import tpu as pltpu
from jax.sharding import PartitionSpec as P


ROWS, COLS, CH = 4, 256, 128
PIX = ROWS * COLS


def over_a(x):
    return x ^ 1


def over_b(x):
    return (x + 1 if x % 2 else x - 1) % 4


def move(block, partner):
    pairs = []
    for chan in range(8):
        for tile in range(32):
            x, y, hi, z, core = partner(chan // 2, chan % 2, tile // 16, (tile // 2) % 8, tile % 2)
            pairs.append((chan * 32 + tile, (2 * x + y) * 32 + (hi * 8 + z % 8) * 2 + core))
    return lax.ppermute(block, ("chan", "tile"), pairs)


def to_y(x, y, hi, z, core):
    return x, 1 - y, hi, z, core


def to_l(x, y, hi, z, core):
    return (over_b(x) if core else over_a(x)), y, hi, z, core


def to_m(x, y, hi, z, core):
    return (over_a(x) if core else over_b(x)), y, hi, z, core


def to_hi(x, y, hi, z, core):
    return x, y, 1 - hi, z, core


def to_core(x, y, hi, z, core):
    return x, y, hi, z, 1 - core


def to_next(x, y, hi, z, core):
    return x, y, hi, (z - 1 if core else z + 1), core


TAPS = (((0, 0), (0, 1)), ((0, 2), (2, 0)), ((2, 1), (2, 2)), ((1, 0), (1, 1)), ((1, 2),))


def add_taps(pixels, filters, acc, base=None):
    def put(b, begin, value, add):
        rows = slice(begin, begin + value.shape[0])
        before = acc if add else base
        acc[b, rows, :] = value if before is None else before[b, rows, :] + value

    for taps in TAPS:
        columns = [filters[3 * a + b] for a, b in taps]
        rhs = jnp.concatenate(columns, axis=1) if len(taps) > 1 else columns[0]
        result = jnp.dot(pixels(), rhs, preferred_element_type=jnp.float32)
        for at, (a, b) in enumerate(taps):
            part = result[:, at * CH : (at + 1) * CH]
            if a == 0:
                put(b, 512, part, False)
            elif a == 2:
                put(b, 0, part[0:512], False)
                put(b, 512, part[512:1024], True)
            else:
                put(b, 256, part, True)


class Copies:
    def __init__(self, sems):
        self.sems, self.started = sems, []

    def start(self, src, dst):
        copy = pltpu.make_async_copy(src, dst, self.sems.at[len(self.started)])
        copy.start()
        self.started.append(copy)

    def wait(self):
        for copy in self.started:
            copy.wait()


def pair_at(pair, z):
    ahead = ((pair - z // 2) * (1 - 2 * (z % 2)) + 8) % 4
    return (ahead % 3 + 1) * ((ahead + 3) // 4)


class Filters:
    def __init__(self, target):
        self.target = target
        tile = lax.axis_index("tile")
        self.y_hi, self.z, self.core = tile // 16, (tile // 2) % 8, tile % 2
        self.partner_back = (self.core + self.z) % 2 == 1

    def place(self, arrays, odd, first, core):
        for piece in range(4):
            half, at_core = (self.y_hi + piece // 2) % 2, (core + piece) % 2
            row = first + half * CH + odd * 64 + at_core * 32
            rows = pl.ds(pl.multiple_of(row, 32), 32)
            array, offset = arrays[piece // 2]
            begin = offset + 9 * (piece % 2)
            self.target[:, rows, :] = array[begin : begin + 9]

    def place_one(self, mine, others, towards_partner, odd, first):
        use_mine = self.partner_back == towards_partner
        pl.when(use_mine)(lambda: self.place(mine, odd, first, self.core))
        pl.when(jnp.logical_not(use_mine))(lambda: self.place(others, odd, first, 1 - self.core))


def rows_of(first, second, at=0):
    return (first, at), (second, at)


def of_pack(pack, slot):
    return (pack, 36 * slot), (pack, 36 * slot + 18)


def first_kernel(*refs):
    blocks, (a0, g0, a1, g1, a2, g2, o12), small = refs[:8], refs[8:15], refs[15:18]
    (xs, acc, *params), (ws, sems) = refs[18:23], refs[23:]
    chan = lax.axis_index("chan")
    x, y = chan // 2, chan % 2
    copies = Copies(sems)
    for source, target in zip(small, params):
        copies.start(source, target)
    filters = Filters(ws)
    z, core = filters.z, filters.core
    turn = 1 - 2 * ((x + core) % 2)
    xl, xm, xf = (x + turn + 4) % 4, (x - turn + 4) % 4, (x + 2) % 4
    places = ((x, y), (x, 1 - y), (xl, y), (xm, y), (xl, 1 - y), (xf, y), (xm, 1 - y), (xf, 1 - y))
    for block, (at_x, at_y) in zip(blocks, places):
        index = 2 * at_x + at_y
        at = 2 * pair_at(index % 4, z) + index // 4
        columns = pl.ds(pl.multiple_of(at * CH, CH), CH)
        xs[:, columns] = block[...]
    even, odd = z % 2, 1 - z % 2
    filters.place(rows_of(a0, g0), even, 0, core)
    filters.place_one(rows_of(a1, g1), of_pack(o12, 0), True, odd, 0)
    filters.place_one(rows_of(a1, g1), of_pack(o12, 0), False, odd, 2 * CH)
    filters.place_one(rows_of(a2, g2), of_pack(o12, 1), False, even, 2 * CH)
    add_taps(lambda: xs[:, 0 : 4 * CH], ws, acc)
    copies.wait()


def second_kernel(xs, base, a2, g2, a3, g3, o12, o3, acc, ws):
    filters = Filters(ws)
    even, odd = filters.z % 2, 1 - filters.z % 2
    filters.place_one(rows_of(a2, g2), of_pack(o12, 1), True, even, 0)
    filters.place_one(rows_of(a3, g3), of_pack(o3, 0), True, odd, 0)
    add_taps(lambda: xs[:, 4 * CH : 6 * CH], ws, acc, base)


def third_kernel(xs, base, a3, g3, o3, a4, g4, bias, outer, inner, mid, own, ws, acc):
    filters = Filters(ws)
    core, even, odd = filters.core, filters.z % 2, 1 - filters.z % 2
    filters.place_one(rows_of(a3, g3), of_pack(o3, 0), False, odd, 0)
    filters.place(rows_of(a4, g4), even, 0, core)
    add_taps(lambda: xs[:, 6 * CH : 8 * CH], ws, acc, base)

    column = lax.broadcasted_iota(jnp.int32, (COLS, CH), 0)

    def row_sum(row):
        rows = pl.ds(pl.multiple_of((row + 1 + core * (3 - 2 * row)) * COLS, COLS), COLS)
        total = [acc[b, rows, :] for b in range(3)]
        left = jnp.where(column == 0, 0.0, pltpu.roll(total[0], 1, 0))
        right = jnp.where(column == COLS - 1, 0.0, pltpu.roll(total[2], COLS - 1, 0))
        return total[1] + left + right

    for slot, row in enumerate((-1, 0, 4, 3)):
        value = row_sum(row)
        own[slot] = value
        if slot < 2:
            outer[slot] = value.astype(jnp.bfloat16)
        else:
            inner[slot - 2] = value.astype(jnp.bfloat16)
    for slot, row in enumerate((1, 2)):
        value = jnp.maximum(row_sum(row) + bias[...], 0.0).astype(jnp.bfloat16)
        mid[slot] = value
        outer[2 + slot] = value
        inner[3 - slot] = value


def add_depth(rows, first, weight, hidden, begin, finish):
    core = lax.axis_index("tile") % 2
    pad = jnp.zeros((len(rows), 8, CH), jnp.float32)
    hidden[:, 0:8, :] = pad
    hidden[:, 264:272, :] = pad
    for at, value in enumerate(rows):
        hidden[at, 8:264, :] = value
    width = 32

    def strip(step, _):
        start = pl.multiple_of(step * width, width)
        sums = [begin(row, pl.ds(start, width)) for row in range(ROWS)]
        for at in range(len(rows)):
            for b in range(7):
                value = hidden[at, pl.ds(start + (5 + b), width), :]
                for row in range(ROWS):
                    a = first + at - row + 3
                    if 0 <= a < 7:
                        sums[row] = sums[row] + value * weight[a + core * (6 - 2 * a), b : b + 1, :]
        for row in range(ROWS):
            finish(row, pl.ds(start, width), sums[row])
        return 0

    lax.fori_loop(0, COLS // width, strip, 0)


def activate(value, bias):
    return jnp.maximum(value + bias[...], 0.0).astype(jnp.bfloat16).astype(jnp.float32)


def depth_early_kernel(own, mid, inner, bias, depth_bias, weight, part, hidden):
    f32 = jnp.float32
    rows = (
        mid[0].astype(f32),
        mid[1].astype(f32),
        activate(own[3] + inner[0].astype(f32), bias),
        activate(inner[1].astype(f32) + own[2], bias),
        inner[2].astype(f32),
        inner[3].astype(f32),
    )

    def finish(row, columns, value):
        part[row, columns, :] = value

    add_depth(
        rows, 1, weight, hidden,
        lambda row, columns: jnp.zeros((columns.size, CH), f32) + depth_bias[...], finish,
    )


def depth_late_kernel(part, own, outer, bias, weight, out, hidden):
    f32 = jnp.float32
    tile = lax.axis_index("tile")
    core = tile % 2
    inside = jnp.logical_and(tile > 0, tile < 31).astype(f32)
    rows = (
        outer[3].astype(f32) * inside,
        outer[2].astype(f32) * inside,
        activate(outer[1].astype(f32) + own[0], bias) * inside,
        activate(own[1] + outer[0].astype(f32), bias),
    )

    def finish(row, columns, value):
        out[row + core * (3 - 2 * row), columns, :] = value.astype(jnp.bfloat16)

    add_depth(rows, -3, weight, hidden, lambda row, columns: part[row, columns, :], finish)


def pack_kernel(mine, others, both):
    both[0:9] = mine[...]
    both[9:18] = others[...]


def gather_all(pixels, weight):
    p0 = pixels.reshape(PIX, CH)
    w0 = weight.reshape(9, 32, CH)
    h0 = move(w0, to_hi)
    w0_other = move(w0, to_core)
    p_y, p_l, p_m = move(p0, to_y), move(p0, to_l), move(p0, to_m)
    a0 = pl.pallas_call(
        pack_kernel,
        out_shape=jax.ShapeDtypeStruct((18, 32, CH), jnp.bfloat16),
        in_specs=[pl.BlockSpec(memory_space=pltpu.VMEM)] * 2,
        out_specs=pl.BlockSpec(memory_space=pltpu.VMEM),
        compiler_params=pltpu.CompilerParams(vmem_limit_bytes=2 << 20),
        name="pack",
    )(w0, w0_other)
    a1 = move(a0, to_next)
    g0 = jnp.concatenate([h0, move(h0, to_core)])
    g1 = move(g0, to_next)
    a2, g2 = move(a1, to_next), move(g1, to_next)
    p_ly, p_ml, p_ym = move(p_l, to_y), move(p_m, to_l), move(p_y, to_m)
    a3, g3 = move(a2, to_next), move(g2, to_next)
    both = jnp.concatenate([a1, g1, a2, g2])
    o12 = move(both, to_core)
    p_far = move(p_ym, to_l)
    a4, g4 = move(a3, to_next), move(g3, to_next)
    both = jnp.concatenate([a3, g3])
    o3 = move(both, to_core)
    blocks = (p0, p_y, p_l, p_m, p_ly, p_ml, p_ym, p_far)
    return blocks, (a0, g0, a1, g1, a2, g2, a3, g3, a4, g4), o12, o3


def in_hbm(array):
    return pltpu.with_memory_space_constraint(array, pltpu.HBM)


def body(pixels, conv_weight, conv_bias, depth_weight, depth_bias):
    vmem = pl.BlockSpec(memory_space=pltpu.VMEM)
    hbm = pl.BlockSpec(memory_space=pltpu.HBM)
    f32, bf16 = jnp.float32, jnp.bfloat16
    message = jax.ShapeDtypeStruct((4, COLS, CH), bf16)
    sums = jax.ShapeDtypeStruct((3, 6 * COLS, CH), f32)

    def settings(blocks):
        return dict(
            compiler_params=pltpu.CompilerParams(vmem_limit_bytes=30 << 20),
            cost_estimate=pl.CostEstimate(
                flops=2 * PIX * 9 * blocks * CH * CH, bytes_accessed=4 << 20, transcendentals=0
            ),
        )

    blocks, filters, o12, o3 = gather_all(pixels, conv_weight)
    xs, acc, *params = pl.pallas_call(
        first_kernel,
        out_shape=(
            jax.ShapeDtypeStruct((PIX, 8 * CH), bf16),
            sums,
            jax.ShapeDtypeStruct((1, CH), f32),
            jax.ShapeDtypeStruct((1, CH), f32),
            jax.ShapeDtypeStruct((7, 7, CH), f32),
        ),
        in_specs=[vmem] * 15 + [hbm] * 3,
        out_specs=(vmem,) * 5,
        scratch_shapes=[pltpu.VMEM((9, 4 * CH, CH), bf16), pltpu.SemaphoreType.DMA((3,))],
        name="first",
        **settings(4),
    )(
        *blocks, *filters[:6], o12,
        in_hbm(conv_bias.reshape(1, CH)),
        in_hbm(depth_bias.reshape(1, CH)),
        in_hbm(depth_weight),
    )
    acc = pl.pallas_call(
        second_kernel,
        out_shape=sums,
        in_specs=[vmem] * 8,
        out_specs=vmem,
        scratch_shapes=[pltpu.VMEM((9, 2 * CH, CH), bf16)],
        name="second",
        **settings(2),
    )(xs, acc, *filters[4:8], o12, o3)
    outer, inner, mid, own = pl.pallas_call(
        third_kernel,
        out_shape=(
            message,
            message,
            jax.ShapeDtypeStruct((2, COLS, CH), bf16),
            jax.ShapeDtypeStruct((4, COLS, CH), f32),
        ),
        in_specs=[vmem] * 8,
        out_specs=(vmem,) * 4,
        scratch_shapes=[
            pltpu.VMEM((9, 2 * CH, CH), bf16),
            pltpu.VMEM((3, 6 * COLS, CH), f32),
        ],
        name="third",
        **settings(2),
    )(xs, acc, *filters[6:8], o3, *filters[8:], params[0])
    bias, depth_bias, weight = params
    across = [(i, i + 1) for i in range(1, 31, 2)]
    from_outer = lax.ppermute(outer, "tile", across + [(j, i) for i, j in across])
    from_inner = lax.ppermute(inner, "tile", [(i, i ^ 1) for i in range(32)])
    part = depth(depth_early_kernel, f32, 6, own, mid, from_inner, bias, depth_bias, weight)
    return depth(depth_late_kernel, bf16, 4, part, own, from_outer, bias, weight)


def depth(kernel, dtype, rows, *operands):
    vmem = pl.BlockSpec(memory_space=pltpu.VMEM)
    return pl.pallas_call(
        kernel,
        out_shape=jax.ShapeDtypeStruct((ROWS, COLS, CH), dtype),
        in_specs=[vmem] * len(operands),
        out_specs=vmem,
        scratch_shapes=[pltpu.VMEM((rows, COLS + 16, CH), jnp.float32)],
        compiler_params=pltpu.CompilerParams(vmem_limit_bytes=20 << 20),
        cost_estimate=pl.CostEstimate(flops=5 * rows * COLS * 49 * CH, bytes_accessed=2 << 20, transcendentals=0),
        name="depth",
    )(*operands)


def solution(mesh):
    in_specs = (
        P("tile", None, "chan"),
        P(None, None, "tile", "chan"),
        P("chan"),
        P(None, None, "chan"),
        P("chan"),
    )
    out_specs = P("tile", None, "chan")
    return jax.shard_map(body, mesh=mesh, in_specs=in_specs, out_specs=out_specs, check_vma=False)
```

```python
import jax
import jax.numpy as jnp
from jax import lax
from jax.experimental import pallas as pl
from jax.experimental.pallas import tpu as pltpu
from jax.sharding import PartitionSpec as P


ROWS, COLS, CH = 4, 256, 128
PIX = ROWS * COLS


def over_a(x):
    return x ^ 1


def over_b(x):
    return (x + 1 if x % 2 else x - 1) % 4


def move(block, partner):
    pairs = []
    for chan in range(8):
        for tile in range(32):
            x, y, hi, z, core = partner(chan // 2, chan % 2, tile // 16, (tile // 2) % 8, tile % 2)
            pairs.append((chan * 32 + tile, (2 * x + y) * 32 + (hi * 8 + z % 8) * 2 + core))
    return lax.ppermute(block, ("chan", "tile"), pairs)


def to_y(x, y, hi, z, core):
    return x, 1 - y, hi, z, core


def to_l(x, y, hi, z, core):
    return (over_b(x) if core else over_a(x)), y, hi, z, core


def to_m(x, y, hi, z, core):
    return (over_a(x) if core else over_b(x)), y, hi, z, core


def to_hi(x, y, hi, z, core):
    return x, y, 1 - hi, z, core


def to_core(x, y, hi, z, core):
    return x, y, hi, z, 1 - core


def to_next(x, y, hi, z, core):
    return x, y, hi, (z - 1 if core else z + 1), core


TAPS = (((0, 0), (0, 1)), ((0, 2), (2, 0)), ((2, 1), (2, 2)), ((1, 0), (1, 1)), ((1, 2),))


def add_taps(pixels, filters, acc, base=None):
    def put(b, begin, value, add):
        rows = slice(begin, begin + value.shape[0])
        before = acc if add else base
        acc[b, rows, :] = value if before is None else before[b, rows, :] + value

    for taps in TAPS:
        columns = [filters[3 * a + b] for a, b in taps]
        rhs = jnp.concatenate(columns, axis=1) if len(taps) > 1 else columns[0]
        result = jnp.dot(pixels(), rhs, preferred_element_type=jnp.float32)
        for at, (a, b) in enumerate(taps):
            part = result[:, at * CH : (at + 1) * CH]
            if a == 0:
                put(b, 512, part, False)
            elif a == 2:
                put(b, 0, part[0:512], False)
                put(b, 512, part[512:1024], True)
            else:
                put(b, 256, part, True)


class Copies:
    def __init__(self, sems):
        self.sems, self.started = sems, []

    def start(self, src, dst):
        copy = pltpu.make_async_copy(src, dst, self.sems.at[len(self.started)])
        copy.start()
        self.started.append(copy)

    def wait(self):
        for copy in self.started:
            copy.wait()


def pair_at(pair, z):
    ahead = ((pair - z // 2) * (1 - 2 * (z % 2)) + 8) % 4
    return (ahead % 3 + 1) * ((ahead + 3) // 4)


class Filters:
    def __init__(self, target):
        self.target = target
        tile = lax.axis_index("tile")
        self.y_hi, self.z, self.core = tile // 16, (tile // 2) % 8, tile % 2
        self.partner_back = (self.core + self.z) % 2 == 1

    def place(self, arrays, odd, first, core):
        for piece in range(4):
            half, at_core = (self.y_hi + piece // 2) % 2, (core + piece) % 2
            row = first + half * CH + odd * 64 + at_core * 32
            rows = pl.ds(pl.multiple_of(row, 32), 32)
            array, offset = arrays[piece // 2]
            begin = offset + 9 * (piece % 2)
            self.target[:, rows, :] = array[begin : begin + 9]

    def place_one(self, mine, others, towards_partner, odd, first):
        use_mine = self.partner_back == towards_partner
        pl.when(use_mine)(lambda: self.place(mine, odd, first, self.core))
        pl.when(jnp.logical_not(use_mine))(lambda: self.place(others, odd, first, 1 - self.core))


def rows_of(first, second, at=0):
    return (first, at), (second, at)


def of_pack(pack, slot):
    return (pack, 36 * slot), (pack, 36 * slot + 18)


def first_kernel(*refs):
    blocks, (a0, g0, a1, g1, a2, g2, o12), small = refs[:8], refs[8:15], refs[15:18]
    (xs, acc, *params), (ws, sems) = refs[18:23], refs[23:]
    chan = lax.axis_index("chan")
    x, y = chan // 2, chan % 2
    copies = Copies(sems)
    for source, target in zip(small, params):
        copies.start(source, target)
    filters = Filters(ws)
    z, core = filters.z, filters.core
    turn = 1 - 2 * ((x + core) % 2)
    xl, xm, xf = (x + turn + 4) % 4, (x - turn + 4) % 4, (x + 2) % 4
    places = ((x, y), (x, 1 - y), (xl, y), (xm, y), (xl, 1 - y), (xf, y), (xm, 1 - y), (xf, 1 - y))
    for block, (at_x, at_y) in zip(blocks, places):
        index = 2 * at_x + at_y
        at = 2 * pair_at(index % 4, z) + index // 4
        columns = pl.ds(pl.multiple_of(at * CH, CH), CH)
        xs[:, columns] = block[...]
    even, odd = z % 2, 1 - z % 2
    filters.place(rows_of(a0, g0), even, 0, core)
    filters.place_one(rows_of(a1, g1), of_pack(o12, 0), True, odd, 0)
    filters.place_one(rows_of(a1, g1), of_pack(o12, 0), False, odd, 2 * CH)
    filters.place_one(rows_of(a2, g2), of_pack(o12, 1), False, even, 2 * CH)
    add_taps(lambda: xs[:, 0 : 4 * CH], ws, acc)
    copies.wait()


def second_kernel(xs, base, a2, g2, a3, g3, o12, o3, acc, ws):
    filters = Filters(ws)
    even, odd = filters.z % 2, 1 - filters.z % 2
    filters.place_one(rows_of(a2, g2), of_pack(o12, 1), True, even, 0)
    filters.place_one(rows_of(a3, g3), of_pack(o3, 0), True, odd, 0)
    add_taps(lambda: xs[:, 4 * CH : 6 * CH], ws, acc, base)


def third_kernel(xs, base, a3, g3, o3, a4, g4, bias, outer, inner, mid, own, ws, acc):
    filters = Filters(ws)
    core, even, odd = filters.core, filters.z % 2, 1 - filters.z % 2
    filters.place_one(rows_of(a3, g3), of_pack(o3, 0), False, odd, 0)
    filters.place(rows_of(a4, g4), even, 0, core)
    add_taps(lambda: xs[:, 6 * CH : 8 * CH], ws, acc, base)

    column = lax.broadcasted_iota(jnp.int32, (COLS, CH), 0)

    def row_sum(row):
        rows = pl.ds(pl.multiple_of((row + 1 + core * (3 - 2 * row)) * COLS, COLS), COLS)
        total = [acc[b, rows, :] for b in range(3)]
        left = jnp.where(column == 0, 0.0, pltpu.roll(total[0], 1, 0))
        right = jnp.where(column == COLS - 1, 0.0, pltpu.roll(total[2], COLS - 1, 0))
        return total[1] + left + right

    for slot, row in enumerate((-1, 0, 4, 3)):
        value = row_sum(row)
        own[slot] = value
        if slot < 2:
            outer[slot] = value.astype(jnp.bfloat16)
        else:
            inner[slot - 2] = value.astype(jnp.bfloat16)
    for slot, row in enumerate((1, 2)):
        value = jnp.maximum(row_sum(row) + bias[...], 0.0).astype(jnp.bfloat16)
        mid[slot] = value
        outer[2 + slot] = value
        inner[3 - slot] = value


def add_depth(rows, first, weight, hidden, begin, finish, after=None, sections=1):
    core = lax.axis_index("tile") % 2
    pad = jnp.zeros((len(rows), 8, CH), jnp.float32)
    hidden[:, 0:8, :] = pad
    hidden[:, 264:272, :] = pad
    for at, value in enumerate(rows):
        hidden[at, 8:264, :] = value
    width = 32

    def strip(step, _):
        start = pl.multiple_of(step * width, width)
        sums = [begin(row, pl.ds(start, width)) for row in range(ROWS)]
        for at in range(len(rows)):
            for b in range(7):
                value = hidden[at, pl.ds(start + (5 + b), width), :]
                for row in range(ROWS):
                    a = first + at - row + 3
                    if 0 <= a < 7:
                        sums[row] = sums[row] + value * weight[a + core * (6 - 2 * a), b : b + 1, :]
        for row in range(ROWS):
            finish(row, pl.ds(start, width), sums[row])
        return 0

    steps = COLS // width // sections
    for section in range(sections):
        lax.fori_loop(section * steps, (section + 1) * steps, strip, 0, unroll=True)
        if after is not None:
            after(pl.ds(section * steps * width, steps * width))


def activate(value, bias):
    return jnp.maximum(value + bias[...], 0.0).astype(jnp.bfloat16).astype(jnp.float32)


def depth_early_kernel(own, mid, inner, bias, depth_bias, weight, part, hidden):
    f32 = jnp.float32
    rows = (
        mid[0].astype(f32),
        mid[1].astype(f32),
        activate(own[3] + inner[0].astype(f32), bias),
        activate(inner[1].astype(f32) + own[2], bias),
        inner[2].astype(f32),
        inner[3].astype(f32),
    )

    def finish(row, columns, value):
        part[row, columns, :] = value

    add_depth(
        rows, 1, weight, hidden,
        lambda row, columns: jnp.zeros((columns.size, CH), f32) + depth_bias[...], finish,
    )


def depth_late_kernel(part, own, outer, bias, weight, out, hidden, done, sems):
    f32 = jnp.float32
    tile = lax.axis_index("tile")
    core = tile % 2
    inside = jnp.logical_and(tile > 0, tile < 31).astype(f32)
    rows = (
        outer[3].astype(f32) * inside,
        outer[2].astype(f32) * inside,
        activate(outer[1].astype(f32) + own[0], bias) * inside,
        activate(own[1] + outer[0].astype(f32), bias),
    )
    copies = Copies(sems)

    def finish(row, columns, value):
        done[row + core * (3 - 2 * row), columns, :] = value.astype(jnp.bfloat16)

    def after(columns):
        copies.start(done.at[:, columns, :], out.at[:, columns, :])

    add_depth(rows, -3, weight, hidden, lambda row, columns: part[row, columns, :], finish, after, 2)
    copies.wait()


def pack_kernel(mine, others, both):
    both[0:9] = mine[...]
    both[9:18] = others[...]


def gather_all(pixels, weight):
    p0 = pixels.reshape(PIX, CH)
    w0 = weight.reshape(9, 32, CH)
    h0 = move(w0, to_hi)
    w0_other = move(w0, to_core)
    p_y, p_l, p_m = move(p0, to_y), move(p0, to_l), move(p0, to_m)
    a0 = pl.pallas_call(
        pack_kernel,
        out_shape=jax.ShapeDtypeStruct((18, 32, CH), jnp.bfloat16),
        in_specs=[pl.BlockSpec(memory_space=pltpu.VMEM)] * 2,
        out_specs=pl.BlockSpec(memory_space=pltpu.VMEM),
        compiler_params=pltpu.CompilerParams(vmem_limit_bytes=2 << 20),
        name="pack",
    )(w0, w0_other)
    a1 = move(a0, to_next)
    g0 = jnp.concatenate([h0, move(h0, to_core)])
    g1 = move(g0, to_next)
    a2, g2 = move(a1, to_next), move(g1, to_next)
    p_ly, p_ml, p_ym = move(p_l, to_y), move(p_m, to_l), move(p_y, to_m)
    a3, g3 = move(a2, to_next), move(g2, to_next)
    both = jnp.concatenate([a1, g1, a2, g2])
    o12 = move(both, to_core)
    p_far = move(p_ym, to_l)
    a4, g4 = move(a3, to_next), move(g3, to_next)
    both = jnp.concatenate([a3, g3])
    o3 = move(both, to_core)
    blocks = (p0, p_y, p_l, p_m, p_ly, p_ml, p_ym, p_far)
    return blocks, (a0, g0, a1, g1, a2, g2, a3, g3, a4, g4), o12, o3


def in_hbm(array):
    return pltpu.with_memory_space_constraint(array, pltpu.HBM)


def body(pixels, conv_weight, conv_bias, depth_weight, depth_bias):
    vmem = pl.BlockSpec(memory_space=pltpu.VMEM)
    hbm = pl.BlockSpec(memory_space=pltpu.HBM)
    f32, bf16 = jnp.float32, jnp.bfloat16
    message = jax.ShapeDtypeStruct((4, COLS, CH), bf16)
    sums = jax.ShapeDtypeStruct((3, 6 * COLS, CH), f32)

    def settings(blocks):
        return dict(
            compiler_params=pltpu.CompilerParams(vmem_limit_bytes=30 << 20),
            cost_estimate=pl.CostEstimate(
                flops=2 * PIX * 9 * blocks * CH * CH, bytes_accessed=4 << 20, transcendentals=0
            ),
        )

    blocks, filters, o12, o3 = gather_all(pixels, conv_weight)
    xs, acc, *params = pl.pallas_call(
        first_kernel,
        out_shape=(
            jax.ShapeDtypeStruct((PIX, 8 * CH), bf16),
            sums,
            jax.ShapeDtypeStruct((1, CH), f32),
            jax.ShapeDtypeStruct((1, CH), f32),
            jax.ShapeDtypeStruct((7, 7, CH), f32),
        ),
        in_specs=[vmem] * 15 + [hbm] * 3,
        out_specs=(vmem,) * 5,
        scratch_shapes=[pltpu.VMEM((9, 4 * CH, CH), bf16), pltpu.SemaphoreType.DMA((3,))],
        name="first",
        **settings(4),
    )(
        *blocks, *filters[:6], o12,
        in_hbm(conv_bias.reshape(1, CH)),
        in_hbm(depth_bias.reshape(1, CH)),
        in_hbm(depth_weight),
    )
    acc = pl.pallas_call(
        second_kernel,
        out_shape=sums,
        in_specs=[vmem] * 8,
        out_specs=vmem,
        scratch_shapes=[pltpu.VMEM((9, 2 * CH, CH), bf16)],
        name="second",
        **settings(2),
    )(xs, acc, *filters[4:8], o12, o3)
    outer, inner, mid, own = pl.pallas_call(
        third_kernel,
        out_shape=(
            message,
            message,
            jax.ShapeDtypeStruct((2, COLS, CH), bf16),
            jax.ShapeDtypeStruct((4, COLS, CH), f32),
        ),
        in_specs=[vmem] * 8,
        out_specs=(vmem,) * 4,
        scratch_shapes=[
            pltpu.VMEM((9, 2 * CH, CH), bf16),
            pltpu.VMEM((3, 6 * COLS, CH), f32),
        ],
        name="third",
        **settings(2),
    )(xs, acc, *filters[6:8], o3, *filters[8:], params[0])
    bias, depth_bias, weight = params
    across = [(i, i + 1) for i in range(1, 31, 2)]
    from_outer = lax.ppermute(outer, "tile", across + [(j, i) for i, j in across])
    from_inner = lax.ppermute(inner, "tile", [(i, i ^ 1) for i in range(32)])
    part = depth(depth_early_kernel, f32, 6, own, mid, from_inner, bias, depth_bias, weight)
    return depth(depth_late_kernel, bf16, 4, part, own, from_outer, bias, weight)


def depth(kernel, dtype, rows, *operands):
    vmem = pl.BlockSpec(memory_space=pltpu.VMEM)
    return pl.pallas_call(
        kernel,
        out_shape=jax.ShapeDtypeStruct((ROWS, COLS, CH), dtype),
        in_specs=[vmem] * len(operands),
        out_specs=vmem if dtype == jnp.float32 else pl.BlockSpec(memory_space=pl.ANY),
        scratch_shapes=[pltpu.VMEM((rows, COLS + 16, CH), jnp.float32)]
        + ([] if dtype == jnp.float32 else [pltpu.VMEM((ROWS, COLS, CH), dtype), pltpu.SemaphoreType.DMA((2,))]),
        compiler_params=pltpu.CompilerParams(vmem_limit_bytes=20 << 20),
        cost_estimate=pl.CostEstimate(flops=5 * rows * COLS * 49 * CH, bytes_accessed=2 << 20, transcendentals=0),
        name="depth",
    )(*operands)


def solution(mesh):
    in_specs = (
        P("tile", None, "chan"),
        P(None, None, "tile", "chan"),
        P("chan"),
        P(None, None, "chan"),
        P("chan"),
    )
    out_specs = P("tile", None, "chan")
    return jax.shard_map(body, mesh=mesh, in_specs=in_specs, out_specs=out_specs, check_vma=False)
```

```python
import jax
import jax.numpy as jnp
from jax import lax
from jax.experimental import pallas as pl
from jax.experimental.pallas import tpu as pltpu
from jax.sharding import PartitionSpec as P


ROWS, COLS, CH = 4, 256, 128
PIX = ROWS * COLS


def over_a(x):
    return x ^ 1


def over_b(x):
    return (x + 1 if x % 2 else x - 1) % 4


def move(block, partner):
    pairs = []
    for chan in range(8):
        for tile in range(32):
            x, y, hi, z, core = partner(chan // 2, chan % 2, tile // 16, (tile // 2) % 8, tile % 2)
            pairs.append((chan * 32 + tile, (2 * x + y) * 32 + (hi * 8 + z % 8) * 2 + core))
    return lax.ppermute(block, ("chan", "tile"), pairs)


def to_y(x, y, hi, z, core):
    return x, 1 - y, hi, z, core


def to_l(x, y, hi, z, core):
    return (over_b(x) if core else over_a(x)), y, hi, z, core


def to_m(x, y, hi, z, core):
    return (over_a(x) if core else over_b(x)), y, hi, z, core


def to_hi(x, y, hi, z, core):
    return x, y, 1 - hi, z, core


def to_core(x, y, hi, z, core):
    return x, y, hi, z, 1 - core


def to_next(x, y, hi, z, core):
    return x, y, hi, (z + 1 if core else z - 1), core


TAPS = (((0, 0), (0, 1)), ((0, 2), (2, 0)), ((2, 1), (2, 2)), ((1, 0), (1, 1)), ((1, 2),))


def add_taps(pixels, filters, acc, base=None):
    def put(b, begin, value, add):
        rows = slice(begin, begin + value.shape[0])
        before = acc if add else base
        acc[b, rows, :] = value if before is None else before[b, rows, :] + value

    for taps in TAPS:
        columns = [filters[3 * a + b] for a, b in taps]
        rhs = jnp.concatenate(columns, axis=1) if len(taps) > 1 else columns[0]
        result = jnp.dot(pixels(), rhs, preferred_element_type=jnp.float32)
        for at, (a, b) in enumerate(taps):
            part = result[:, at * CH : (at + 1) * CH]
            if a == 0:
                put(b, 512, part, False)
            elif a == 2:
                put(b, 0, part[0:512], False)
                put(b, 512, part[512:1024], True)
            else:
                put(b, 256, part, True)


class Copies:
    def __init__(self, sems):
        self.sems, self.started = sems, []

    def start(self, src, dst):
        copy = pltpu.make_async_copy(src, dst, self.sems.at[len(self.started)])
        copy.start()
        self.started.append(copy)

    def wait(self):
        for copy in self.started:
            copy.wait()


def pair_at(pair, z):
    ahead = ((pair - z // 2) * (1 - 2 * (z % 2)) + 8) % 4
    return (ahead % 3 + 1) * ((ahead + 3) // 4)


class Filters:
    def __init__(self, target):
        self.target = target
        tile = lax.axis_index("tile")
        self.y_hi, self.z, self.core = tile // 16, (tile // 2) % 8, tile % 2
        self.partner_back = (self.core + self.z) % 2 == 0

    def place(self, arrays, odd, first, core):
        for piece in range(4):
            half, at_core = (self.y_hi + piece // 2) % 2, (core + piece) % 2
            row = first + half * CH + odd * 64 + at_core * 32
            rows = pl.ds(pl.multiple_of(row, 32), 32)
            array, offset = arrays[piece // 2]
            begin = offset + 9 * (piece % 2)
            self.target[:, rows, :] = array[begin : begin + 9]

    def place_one(self, mine, others, towards_partner, odd, first):
        use_mine = self.partner_back == towards_partner
        pl.when(use_mine)(lambda: self.place(mine, odd, first, self.core))
        pl.when(jnp.logical_not(use_mine))(lambda: self.place(others, odd, first, 1 - self.core))


def rows_of(first, second, at=0):
    return (first, at), (second, at)


def of_pack(pack, slot):
    return (pack, 36 * slot), (pack, 36 * slot + 18)


def first_kernel(*refs):
    blocks, (a0, g0, a1, g1, a2, g2, o12), small = refs[:8], refs[8:15], refs[15:18]
    (xs, acc, *params), (ws, sems) = refs[18:23], refs[23:]
    chan = lax.axis_index("chan")
    x, y = chan // 2, chan % 2
    copies = Copies(sems)
    for source, target in zip(small, params):
        copies.start(source, target)
    filters = Filters(ws)
    z, core = filters.z, filters.core
    turn = 1 - 2 * ((x + core) % 2)
    xl, xm, xf = (x + turn + 4) % 4, (x - turn + 4) % 4, (x + 2) % 4
    places = ((x, y), (x, 1 - y), (xl, y), (xm, y), (xl, 1 - y), (xf, y), (xm, 1 - y), (xf, 1 - y))
    for block, (at_x, at_y) in zip(blocks, places):
        index = 2 * at_x + at_y
        at = 2 * pair_at(index % 4, z) + index // 4
        columns = pl.ds(pl.multiple_of(at * CH, CH), CH)
        xs[:, columns] = block[...]
    even, odd = z % 2, 1 - z % 2
    filters.place(rows_of(a0, g0), even, 0, core)
    filters.place_one(rows_of(a1, g1), of_pack(o12, 0), True, odd, 0)
    filters.place_one(rows_of(a1, g1), of_pack(o12, 0), False, odd, 2 * CH)
    filters.place_one(rows_of(a2, g2), of_pack(o12, 1), False, even, 2 * CH)
    add_taps(lambda: xs[:, 0 : 4 * CH], ws, acc)
    copies.wait()


def second_kernel(xs, base, a2, g2, a3, g3, o12, o3, acc, ws):
    filters = Filters(ws)
    even, odd = filters.z % 2, 1 - filters.z % 2
    filters.place_one(rows_of(a2, g2), of_pack(o12, 1), True, even, 0)
    filters.place_one(rows_of(a3, g3), of_pack(o3, 0), True, odd, 0)
    add_taps(lambda: xs[:, 4 * CH : 6 * CH], ws, acc, base)


def third_kernel(xs, base, a3, g3, o3, a4, g4, bias, outer, inner, mid, own, ws, acc):
    filters = Filters(ws)
    core, even, odd = filters.core, filters.z % 2, 1 - filters.z % 2
    filters.place_one(rows_of(a3, g3), of_pack(o3, 0), False, odd, 0)
    filters.place(rows_of(a4, g4), even, 0, core)
    add_taps(lambda: xs[:, 6 * CH : 8 * CH], ws, acc, base)

    column = lax.broadcasted_iota(jnp.int32, (COLS, CH), 0)

    def row_sum(row):
        rows = pl.ds(pl.multiple_of((row + 1 + core * (3 - 2 * row)) * COLS, COLS), COLS)
        total = [acc[b, rows, :] for b in range(3)]
        left = jnp.where(column == 0, 0.0, pltpu.roll(total[0], 1, 0))
        right = jnp.where(column == COLS - 1, 0.0, pltpu.roll(total[2], COLS - 1, 0))
        return total[1] + left + right

    for slot, row in enumerate((-1, 0, 4, 3)):
        value = row_sum(row)
        own[slot] = value
        if slot < 2:
            outer[slot] = value.astype(jnp.bfloat16)
        else:
            inner[slot - 2] = value.astype(jnp.bfloat16)
    for slot, row in enumerate((1, 2)):
        value = jnp.maximum(row_sum(row) + bias[...], 0.0).astype(jnp.bfloat16)
        mid[slot] = value
        outer[2 + slot] = value
        inner[3 - slot] = value


def add_depth(rows, first, weight, hidden, begin, finish):
    core = lax.axis_index("tile") % 2
    pad = jnp.zeros((len(rows), 8, CH), jnp.float32)
    hidden[:, 0:8, :] = pad
    hidden[:, 264:272, :] = pad
    for at, value in enumerate(rows):
        hidden[at, 8:264, :] = value
    width = 32

    def strip(step, _):
        start = pl.multiple_of(step * width, width)
        sums = [begin(row, pl.ds(start, width)) for row in range(ROWS)]
        for at in range(len(rows)):
            for b in range(7):
                value = hidden[at, pl.ds(start + (5 + b), width), :]
                for row in range(ROWS):
                    a = first + at - row + 3
                    if 0 <= a < 7:
                        sums[row] = sums[row] + value * weight[a + core * (6 - 2 * a), b : b + 1, :]
        for row in range(ROWS):
            finish(row, pl.ds(start, width), sums[row])
        return 0

    lax.fori_loop(0, COLS // width, strip, 0, unroll=True)


def activate(value, bias):
    return jnp.maximum(value + bias[...], 0.0).astype(jnp.bfloat16).astype(jnp.float32)


def depth_early_kernel(own, mid, inner, bias, depth_bias, weight, part, hidden):
    f32 = jnp.float32
    rows = (
        mid[0].astype(f32),
        mid[1].astype(f32),
        activate(own[3] + inner[0].astype(f32), bias),
        activate(inner[1].astype(f32) + own[2], bias),
        inner[2].astype(f32),
        inner[3].astype(f32),
    )

    def finish(row, columns, value):
        part[row, columns, :] = value

    add_depth(
        rows, 1, weight, hidden,
        lambda row, columns: jnp.zeros((columns.size, CH), f32) + depth_bias[...], finish,
    )


def depth_late_kernel(part, own, outer, bias, weight, out, hidden):
    f32 = jnp.float32
    tile = lax.axis_index("tile")
    core = tile % 2
    inside = jnp.logical_and(tile > 0, tile < 31).astype(f32)
    rows = (
        outer[3].astype(f32) * inside,
        outer[2].astype(f32) * inside,
        activate(outer[1].astype(f32) + own[0], bias) * inside,
        activate(own[1] + outer[0].astype(f32), bias),
    )

    def finish(row, columns, value):
        out[row + core * (3 - 2 * row), columns, :] = value.astype(jnp.bfloat16)

    add_depth(rows, -3, weight, hidden, lambda row, columns: part[row, columns, :], finish)


def pack_kernel(mine, others, both):
    both[0:9] = mine[...]
    both[9:18] = others[...]


def gather_all(pixels, weight):
    p0 = pixels.reshape(PIX, CH)
    w0 = weight.reshape(9, 32, CH)
    h0 = move(w0, to_hi)
    w0_other = move(w0, to_core)
    p_y, p_l, p_m = move(p0, to_y), move(p0, to_l), move(p0, to_m)
    a0 = pl.pallas_call(
        pack_kernel,
        out_shape=jax.ShapeDtypeStruct((18, 32, CH), jnp.bfloat16),
        in_specs=[pl.BlockSpec(memory_space=pltpu.VMEM)] * 2,
        out_specs=pl.BlockSpec(memory_space=pltpu.VMEM),
        compiler_params=pltpu.CompilerParams(vmem_limit_bytes=2 << 20),
        name="pack",
    )(w0, w0_other)
    a1 = move(a0, to_next)
    g0 = jnp.concatenate([h0, move(h0, to_core)])
    g1 = move(g0, to_next)
    a2, g2 = move(a1, to_next), move(g1, to_next)
    p_ly, p_ml, p_ym = move(p_l, to_y), move(p_m, to_l), move(p_y, to_m)
    a3, g3 = move(a2, to_next), move(g2, to_next)
    both = jnp.concatenate([a1, g1, a2, g2])
    o12 = move(both, to_core)
    p_far = move(p_ym, to_l)
    a4, g4 = move(a3, to_next), move(g3, to_next)
    both = jnp.concatenate([a3, g3])
    o3 = move(both, to_core)
    blocks = (p0, p_y, p_l, p_m, p_ly, p_ml, p_ym, p_far)
    return blocks, (a0, g0, a1, g1, a2, g2, a3, g3, a4, g4), o12, o3


def in_hbm(array):
    return pltpu.with_memory_space_constraint(array, pltpu.HBM)


def body(pixels, conv_weight, conv_bias, depth_weight, depth_bias):
    vmem = pl.BlockSpec(memory_space=pltpu.VMEM)
    hbm = pl.BlockSpec(memory_space=pltpu.HBM)
    f32, bf16 = jnp.float32, jnp.bfloat16
    message = jax.ShapeDtypeStruct((4, COLS, CH), bf16)
    sums = jax.ShapeDtypeStruct((3, 6 * COLS, CH), f32)

    def settings(blocks):
        return dict(
            compiler_params=pltpu.CompilerParams(vmem_limit_bytes=30 << 20),
            cost_estimate=pl.CostEstimate(
                flops=2 * PIX * 9 * blocks * CH * CH, bytes_accessed=4 << 20, transcendentals=0
            ),
        )

    blocks, filters, o12, o3 = gather_all(pixels, conv_weight)
    xs, acc, *params = pl.pallas_call(
        first_kernel,
        out_shape=(
            jax.ShapeDtypeStruct((PIX, 8 * CH), bf16),
            sums,
            jax.ShapeDtypeStruct((1, CH), f32),
            jax.ShapeDtypeStruct((1, CH), f32),
            jax.ShapeDtypeStruct((7, 7, CH), f32),
        ),
        in_specs=[vmem] * 15 + [hbm] * 3,
        out_specs=(vmem,) * 5,
        scratch_shapes=[pltpu.VMEM((9, 4 * CH, CH), bf16), pltpu.SemaphoreType.DMA((3,))],
        name="first",
        **settings(4),
    )(
        *blocks, *filters[:6], o12,
        in_hbm(conv_bias.reshape(1, CH)),
        in_hbm(depth_bias.reshape(1, CH)),
        in_hbm(depth_weight),
    )
    acc = pl.pallas_call(
        second_kernel,
        out_shape=sums,
        in_specs=[vmem] * 8,
        out_specs=vmem,
        scratch_shapes=[pltpu.VMEM((9, 2 * CH, CH), bf16)],
        name="second",
        **settings(2),
    )(xs, acc, *filters[4:8], o12, o3)
    outer, inner, mid, own = pl.pallas_call(
        third_kernel,
        out_shape=(
            message,
            message,
            jax.ShapeDtypeStruct((2, COLS, CH), bf16),
            jax.ShapeDtypeStruct((4, COLS, CH), f32),
        ),
        in_specs=[vmem] * 8,
        out_specs=(vmem,) * 4,
        scratch_shapes=[
            pltpu.VMEM((9, 2 * CH, CH), bf16),
            pltpu.VMEM((3, 6 * COLS, CH), f32),
        ],
        name="third",
        **settings(2),
    )(xs, acc, *filters[6:8], o3, *filters[8:], params[0])
    bias, depth_bias, weight = params
    across = [(i, i + 1) for i in range(1, 31, 2)]
    from_outer = lax.ppermute(outer, "tile", across + [(j, i) for i, j in across])
    from_inner = lax.ppermute(inner, "tile", [(i, i ^ 1) for i in range(32)])
    part = depth(depth_early_kernel, f32, 6, own, mid, from_inner, bias, depth_bias, weight)
    return depth(depth_late_kernel, bf16, 4, part, own, from_outer, bias, weight)


def depth(kernel, dtype, rows, *operands):
    vmem = pl.BlockSpec(memory_space=pltpu.VMEM)
    return pl.pallas_call(
        kernel,
        out_shape=jax.ShapeDtypeStruct((ROWS, COLS, CH), dtype),
        in_specs=[vmem] * len(operands),
        out_specs=vmem,
        scratch_shapes=[pltpu.VMEM((rows, COLS + 16, CH), jnp.float32)],
        compiler_params=pltpu.CompilerParams(vmem_limit_bytes=20 << 20),
        cost_estimate=pl.CostEstimate(flops=5 * rows * COLS * 49 * CH, bytes_accessed=2 << 20, transcendentals=0),
        name="depth",
    )(*operands)


def solution(mesh):
    in_specs = (
        P("tile", None, "chan"),
        P(None, None, "tile", "chan"),
        P("chan"),
        P(None, None, "chan"),
        P("chan"),
    )
    out_specs = P("tile", None, "chan")
    return jax.shard_map(body, mesh=mesh, in_specs=in_specs, out_specs=out_specs, check_vma=False)
```
